32 devices in a mesh: frow: 4 (over x, core), fcol: 8 (over z, y).
Axes of the slice: x: 2, y: 2, z: 4, core: 2. Of those that a mesh axis runs over, the one named last changes fastest.
Arguments:
- facet_image: bfloat16 [2048, 4096], P('frow', 'fcol'), may hold values from -6 to 6
- row_offsets: int32 [2], replicated, may hold values from 0 to 65280
- col_offsets: int32 [2], replicated, may hold values from 0 to 65280
- vis_subgrid: int32 [16384], P(('frow', 'fcol')), may hold values from 0 to 3
- vis_u: int32 [16384], P(('frow', 'fcol')), may hold values from 0 to 255
- vis_v: int32 [16384], P(('frow', 'fcol')), may hold values from 0 to 255
- observed: float32 [2, 16384], P(None, ('frow', 'fcol')), may hold values from -6 to 6
Outputs:
- facet_residual: float32 [2048, 4096], P('frow', 'fcol')
- residual_vis: float32 [2, 16384], P(None, ('frow', 'fcol'))
The draws below stay inside these ranges and needn't reach their ends.
Inputs may be any that keep to these rules, and one draw needn't show every extreme that they name: `vis_subgrid`: subgrid numbers count row by row over the 2 x 2 subgrids.
All inputs are finite; a program needn't handle non-finite values.
Results may differ from the reference program's by a relative error of at most 0.023.
Values may be sent and summed in bfloat16 or wider, within the bound.
A program may use at most 64 MiB of HBM per device.

```python
import math
import jax
import jax.numpy as jnp
import numpy as np
from jax import lax

SKY = 65536
FS = 512
SG = 256
NR = 2
NC = 2
NVIS = 16384
N_FROW = 4
N_FCOL = 8


def with_ends(drawn, rng, least, largest):
    index_at = [jax.random.randint(jax.random.fold_in(rng, axis), (), 0, length) for axis, length in enumerate(drawn.shape)]
    main_axis = drawn.shape.index(max(drawn.shape))
    next_to = index_at[:main_axis] + [(index_at[main_axis] + 1) % drawn.shape[main_axis]] + index_at[main_axis + 1:]
    return drawn.at[tuple(index_at)].set(least).at[tuple(next_to)].set(largest)


def block_levels(key, extent, split, low, largest):
    loudness = 1.0
    for dim, parts in split:
        heights = jax.random.uniform(jax.random.fold_in(jax.random.fold_in(key, 6), dim), (parts,), jnp.float32, low / len(split), largest / len(split))
        loudness = loudness * jnp.repeat(jnp.exp(heights), extent[dim] // parts).reshape((-1,) + (1,) * (len(extent) - 1 - dim))
    return loudness


def rank_table(number_of, slope):
    loads = [(1 << 20) // math.isqrt(rank ** slope) + 1 for rank in range(1, number_of + 1)]
    deviation = 1 + sum(loads) // (1 << 30)
    return np.cumsum(np.array([max(1, weight // deviation) for weight in loads]))


def ranked(key, shape, amount, lean):
    table = rank_table(amount, lean)
    pick = jax.random.randint(jax.random.fold_in(key, 1), shape, 0, int(table[amount - 1]))
    standing = jnp.searchsorted(jnp.asarray(table, jnp.int32), pick, side="right")
    return jax.random.permutation(jax.random.fold_in(key, 2), amount)[standing].astype(jnp.int32)


def scatter_about(stream_key, dims, deviation, bound, pieces=(), kind=jnp.bfloat16):
    values = jax.random.normal(stream_key, dims, jnp.float32) * deviation
    if len(pieces) > 0:
        values = block_levels(stream_key, dims, pieces, -0.22, 0.18) * values
    return jnp.clip(values, min=-bound, max=bound).astype(kind)


def setup_inputs(seed: int = 0) -> dict:
    streams_of = jax.random.split(jax.random.key(seed), 8)
    facet_image = scatter_about(streams_of[0], (FS * N_FROW, FS * N_FCOL), 1.0, 6.0, ((0, 4), (1, 8)))
    row_offsets = jax.random.randint(streams_of[1], (NR,), 0, SKY - SG + 1).astype(jnp.int32)
    col_offsets = jax.random.randint(streams_of[2], (NC,), 0, SKY - SG + 1).astype(jnp.int32)
    vis_subgrid = with_ends(ranked(streams_of[3], (NVIS,), NR * NC, 2), jax.random.fold_in(streams_of[3], 3), 0, (NR * NC) - 1).astype(jnp.int32)
    vis_u = with_ends(jax.random.randint(streams_of[4], (NVIS,), 0, SG), jax.random.fold_in(streams_of[4], 1), 0, SG - 1).astype(jnp.int32)
    vis_v = with_ends(jax.random.randint(streams_of[5], (NVIS,), 0, SG), jax.random.fold_in(streams_of[5], 1), 0, SG - 1).astype(jnp.int32)
    observed = scatter_about(streams_of[6], (2, NVIS), 1.0, 6.0, ((1, 32),), jnp.float32)
    return dict(facet_image=facet_image, row_offsets=row_offsets, col_offsets=col_offsets, vis_subgrid=vis_subgrid, vis_u=vis_u, vis_v=vis_v, observed=observed)


def wrapped(frequency, position):
    high_part = frequency // 256
    low_part = frequency % 256
    return (high_part * (position * 256 % SKY) + low_part * position) % SKY

def sky_tables(start, positions):
    frequency = start + jnp.arange(SG, dtype=jnp.int32)[:, None]
    angles = wrapped(frequency, positions[None, :]).astype(jnp.float32) * (2.0 * math.pi / SKY)
    return (jnp.cos(angles).astype(jnp.bfloat16), jnp.sin(angles).astype(jnp.bfloat16))

def grid_tables():
    counter = jnp.arange(SG, dtype=jnp.int32)
    angles = (counter[:, None] * counter[None, :] % SG).astype(jnp.float32) * (2.0 * math.pi / SG)
    return (jnp.cos(angles).astype(jnp.bfloat16), jnp.sin(angles).astype(jnp.bfloat16))

def reference(facet_image, row_offsets, col_offsets, vis_subgrid, vis_u, vis_v, observed):
    f32 = jnp.float32
    hp = lax.Precision.HIGHEST
    scale_in = 1.0 / (FS * math.sqrt(N_FROW * N_FCOL))
    scale_out = 1.0 / (SG * math.sqrt(NR * NC))
    row_pos = (jnp.arange(N_FROW, dtype=jnp.int32)[:, None] * (SKY // N_FROW) + jnp.arange(FS, dtype=jnp.int32)[None, :] * (SKY // (N_FROW * FS))).reshape(-1)
    col_pos = (jnp.arange(N_FCOL, dtype=jnp.int32)[:, None] * (SKY // N_FCOL) + jnp.arange(FS, dtype=jnp.int32)[None, :] * (SKY // (N_FCOL * FS))).reshape(-1)
    row_tabs = [sky_tables(row_offsets[row_pick], row_pos) for row_pick in range(NR)]
    col_tabs = [sky_tables(col_offsets[col_pick], col_pos) for col_pick in range(NC)]
    blocks = facet_image.astype(f32).reshape(N_FROW * FS, N_FCOL, FS)
    col_sums = []
    for col_pick in range(NC):
        cos_tab, sin_tab = col_tabs[col_pick]
        p_full = jnp.einsum('xjy,bjy->xjb', blocks, cos_tab.astype(f32).reshape(SG, N_FCOL, FS)).astype(jnp.bfloat16)
        q_full = jnp.einsum('xjy,bjy->xjb', blocks, sin_tab.astype(f32).reshape(SG, N_FCOL, FS)).astype(jnp.bfloat16)
        col_sums.append((p_full.astype(f32).sum(axis=1), q_full.astype(f32).sum(axis=1)))
    real_list = []
    imag_list = []
    for row_pick in range(NR):
        crow = row_tabs[row_pick][0].astype(f32)
        srow = row_tabs[row_pick][1].astype(f32)
        for col_pick in range(NC):
            psum, qsum = col_sums[col_pick]
            real_list.append((jnp.dot(crow, psum, precision=hp) - jnp.dot(srow, qsum, precision=hp)) * scale_in)
            imag_list.append(-(jnp.dot(crow, qsum, precision=hp) + jnp.dot(srow, psum, precision=hp)) * scale_in)
    sub_real = jnp.stack(real_list).astype(jnp.bfloat16).reshape(NR * NC * SG, SG)
    sub_imag = jnp.stack(imag_list).astype(jnp.bfloat16).reshape(NR * NC * SG, SG)
    kcos, ksin = grid_tables()
    w_real = (jnp.dot(sub_real, kcos, preferred_element_type=f32) - jnp.dot(sub_imag, ksin, preferred_element_type=f32)).astype(jnp.bfloat16)
    w_imag = (jnp.dot(sub_real, ksin, preferred_element_type=f32) + jnp.dot(sub_imag, kcos, preferred_element_type=f32)).astype(jnp.bfloat16)
    w_real = w_real.astype(f32).reshape(NR * NC, SG, SG)
    w_imag = w_imag.astype(f32).reshape(NR * NC, SG, SG)
    kc32 = kcos.astype(f32)
    ks32 = ksin.astype(f32)
    hat_real = (jnp.einsum('au,sav->suv', kc32, w_real) - jnp.einsum('au,sav->suv', ks32, w_imag)) / SG
    hat_imag = (jnp.einsum('au,sav->suv', ks32, w_real) + jnp.einsum('au,sav->suv', kc32, w_imag)) / SG
    cell_ids = ((vis_subgrid * SG + vis_u) * SG + vis_v).astype(jnp.int32)
    model_vis = jnp.stack([hat_real.reshape(-1)[cell_ids], hat_imag.reshape(-1)[cell_ids]])
    residual = observed - model_vis
    cells_all = NR * NC * SG * SG
    ghat_real = jax.ops.segment_sum(residual[0], cell_ids, num_segments=cells_all).astype(jnp.bfloat16).reshape(NR * NC * SG, SG)
    ghat_imag = jax.ops.segment_sum(residual[1], cell_ids, num_segments=cells_all).astype(jnp.bfloat16).reshape(NR * NC * SG, SG)
    v_real = (jnp.dot(ghat_real, kcos, preferred_element_type=f32) + jnp.dot(ghat_imag, ksin, preferred_element_type=f32)).astype(jnp.bfloat16)
    v_imag = (jnp.dot(ghat_imag, kcos, preferred_element_type=f32) - jnp.dot(ghat_real, ksin, preferred_element_type=f32)).astype(jnp.bfloat16)
    v_real = v_real.astype(f32).reshape(NR * NC, SG, SG)
    v_imag = v_imag.astype(f32).reshape(NR * NC, SG, SG)
    back_real = ((jnp.einsum('au,sub->sab', kc32, v_real) + jnp.einsum('au,sub->sab', ks32, v_imag)) / SG).astype(jnp.bfloat16)
    back_imag = ((jnp.einsum('au,sub->sab', kc32, v_imag) - jnp.einsum('au,sub->sab', ks32, v_real)) / SG).astype(jnp.bfloat16)
    image = jnp.zeros((N_FROW * FS, N_FCOL * FS), f32)
    for col_pick in range(NC):
        u_real = jnp.zeros((N_FROW * FS, SG), f32)
        u_imag = jnp.zeros((N_FROW * FS, SG), f32)
        for row_pick in range(NR):
            crow, srow = row_tabs[row_pick]
            sub_index = row_pick * NC + col_pick
            g_real = back_real[sub_index]
            g_imag = back_imag[sub_index]
            u_real = u_real + jnp.dot(crow.T, g_real, preferred_element_type=f32) - jnp.dot(srow.T, g_imag, preferred_element_type=f32)
            u_imag = u_imag + jnp.dot(crow.T, g_imag, preferred_element_type=f32) + jnp.dot(srow.T, g_real, preferred_element_type=f32)
        ccol, scol = col_tabs[col_pick]
        image = image + jnp.dot(u_real.astype(jnp.bfloat16), ccol, preferred_element_type=f32) - jnp.dot(u_imag.astype(jnp.bfloat16), scol, preferred_element_type=f32)
    return (image * scale_out, residual)
```

```python
import functools
import math

import jax
import jax.numpy as jnp
from jax import lax
from jax.experimental import pallas as pl
from jax.experimental.pallas import tpu as pltpu
from jax.sharding import PartitionSpec as P

SKY = 65536
SG = 256
NR = 2
NC = 2
f32 = jnp.float32
bf16 = jnp.bfloat16
i32 = jnp.int32
MESH = pl.DeviceIdType.MESH
VM = pl.BlockSpec(memory_space=pltpu.VMEM)
SM = pl.BlockSpec(memory_space=pltpu.SMEM)
LIMIT = 60 << 20


def geometry():
    rows = lax.axis_size("frow")
    cols = lax.axis_size("fcol")
    nx = rows // 2
    ny = 1 << ((cols.bit_length() - 1) // 2)
    nz = cols // ny
    return rows, cols, nx, ny, nz


def position():
    _, _, _, ny, _ = geometry()
    frow = lax.axis_index("frow")
    fcol = lax.axis_index("fcol")
    return frow // 2, frow % 2, fcol % ny, fcol // ny


def dims(contract):
    return ((contract, contract), ((), ()))


def phase(product):
    angle = (product & (SKY - 1)).astype(f32) * (2.0 * math.pi / SKY)
    return jnp.cos(angle), jnp.sin(angle)


def expand(first, places, c_ref, s_ref):
    n = places.shape[1]
    steps = lax.broadcasted_iota(i32, (16, n), 0)
    c0, s0 = phase(steps * places)
    c1, s1 = phase((first + 16 * steps) * places)
    for k in range(SG // 16):
        ck = c1[k : k + 1]
        sk = s1[k : k + 1]
        c_ref[k * 16 : k * 16 + 16, :] = (ck * c0 - sk * s0).astype(bf16)
        s_ref[k * 16 : k * 16 + 16, :] = (sk * c0 + ck * s0).astype(bf16)


def tables_kernel(fs, ro_ref, co_ref, ar_ref, ai_ref, bt_ref, kk, ks, rc, rs):
    rows, cols, _, _, _ = geometry()
    x, h, _, _ = position()
    expand(0, lax.broadcasted_iota(i32, (1, SG), 1) * (SKY // SG), kk, ks)
    kcos = kk[...]
    ksin = ks[...]

    def compose(n):
        c = rc[:, :n]
        s = rs[:, :n]
        re = jnp.dot(kcos, c, preferred_element_type=f32) + jnp.dot(ksin, s, preferred_element_type=f32)
        im = jnp.dot(ksin, c, preferred_element_type=f32) - jnp.dot(kcos, s, preferred_element_type=f32)
        return re.astype(bf16), im.astype(bf16)

    step = SKY // (cols * fs)
    fcol = lax.axis_index("fcol")
    places = (fcol * fs + lax.broadcasted_iota(i32, (1, fs), 1)) * step
    expand(co_ref[h], places, rc.at[:, :fs], rs.at[:, :fs])
    re, im = compose(fs)
    bt_ref[:SG] = re
    bt_ref[SG:] = im
    step = SKY // (rows * fs)
    places = (x * (2 * fs) + lax.broadcasted_iota(i32, (1, 2 * fs), 1)) * step
    for r in range(NR):
        expand(ro_ref[r], places, rc, rs)
        re, im = compose(2 * fs)
        ar_ref[r * SG : r * SG + SG] = re
        ai_ref[r * SG : r * SG + SG] = im


def tables(fs, ro, co):
    return pl.pallas_call(
        functools.partial(tables_kernel, fs),
        out_shape=[
            jax.ShapeDtypeStruct((NR * SG, 2 * fs), bf16),
            jax.ShapeDtypeStruct((NR * SG, 2 * fs), bf16),
            jax.ShapeDtypeStruct((2 * SG, fs), bf16),
        ],
        in_specs=[SM, SM],
        out_specs=[VM, VM, VM],
        scratch_shapes=[
            pltpu.VMEM((SG, SG), bf16),
            pltpu.VMEM((SG, SG), bf16),
            pltpu.VMEM((SG, 2 * fs), bf16),
            pltpu.VMEM((SG, 2 * fs), bf16),
        ],
        compiler_params=pltpu.CompilerParams(vmem_limit_bytes=LIMIT),
        name="tables",
    )(ro, co)


def everyone(n, cols, me, act):
    def step(d, carry):
        to = lax.rem(me + d, n)
        frm = lax.rem(me - d + n, n)
        act(d, to, frm)
        return carry

    lax.fori_loop(1, n, step, 0)


def greet_all(n, cols, me):
    barrier = pltpu.get_barrier_semaphore()

    def hello(d, to, frm):
        pl.semaphore_signal(barrier, inc=1, device_id=(to // cols, to % cols), device_id_type=MESH)

    everyone(n, cols, me, hello)
    pl.semaphore_wait(barrier, n - 1)


def swap_kernel(facet_ref, vis_ref, pair_ref, all_ref, lsem, ssem, rsem, vs, vr):
    rows, cols, _, _, _ = geometry()
    frow = lax.axis_index("frow")
    fcol = lax.axis_index("fcol")
    h = frow % 2
    n = rows * cols
    me = frow * cols + fcol
    greet_all(n, cols, me)
    sib = frow + 1 - 2 * h
    big = pltpu.make_async_remote_copy(
        facet_ref, pair_ref.at[h], ssem, rsem, device_id=(sib, fcol), device_id_type=MESH
    )
    big.start()

    def link(d, to, slot):
        return pltpu.make_async_remote_copy(
            vis_ref, all_ref.at[slot], vs.at[d], vr.at[d],
            device_id=(to // cols, to % cols), device_id_type=MESH,
        )

    everyone(n, cols, me, lambda d, to, frm: link(d, to, me).start())
    own = pltpu.make_async_copy(facet_ref, pair_ref.at[h], lsem.at[0])
    own.start()
    mine = pltpu.make_async_copy(vis_ref, all_ref.at[me], lsem.at[1])
    mine.start()
    own.wait()
    mine.wait()
    everyone(n, cols, me, lambda d, to, frm: link(d, to, me).wait_send())
    everyone(n, cols, me, lambda d, to, frm: link(d, to, frm).wait_recv())
    big.wait_send()
    pltpu.make_async_remote_copy(
        facet_ref, pair_ref.at[1 - h], ssem, rsem, device_id=(sib, fcol), device_id_type=MESH
    ).wait_recv()


def swap(facet, vis):
    rows, cols, _, _, _ = geometry()
    n = rows * cols
    return pl.pallas_call(
        swap_kernel,
        out_shape=[
            jax.ShapeDtypeStruct((2,) + facet.shape, facet.dtype),
            jax.ShapeDtypeStruct((n,) + vis.shape, vis.dtype),
        ],
        in_specs=[VM, VM],
        out_specs=[VM, VM],
        scratch_shapes=[
            pltpu.SemaphoreType.DMA((2,)),
            pltpu.SemaphoreType.DMA,
            pltpu.SemaphoreType.DMA,
            pltpu.SemaphoreType.DMA((n,)),
            pltpu.SemaphoreType.DMA((n,)),
        ],
        compiler_params=pltpu.CompilerParams(
            collective_id=0, has_side_effects=True, vmem_limit_bytes=LIMIT
        ),
        name="swap",
    )(facet, vis)


def forward_kernel(nx, ny, pair_ref, ar_ref, ai_ref, bt_ref, z_ref, zb_ref):
    fs = pair_ref.shape[1]
    stack = pair_ref[...].reshape(2 * fs, fs)
    p = lax.dot_general(stack, bt_ref[...], (((1,), (1,)), ((), ())), preferred_element_type=f32).astype(bf16)
    part = NR * SG // (nx * ny)
    for b in range(nx * ny):
        cut = slice(b * part, b * part + part)
        one = jnp.dot(ar_ref[cut], p, preferred_element_type=f32)
        two = jnp.dot(ai_ref[cut], p, preferred_element_type=f32)
        zr = one[:, :SG] - two[:, SG:]
        zi = one[:, SG:] + two[:, :SG]
        bx, by = b // ny, b % ny
        z_ref[0, bx, by] = zr
        z_ref[1, bx, by] = zi
        zb_ref[0, bx, by] = zr.astype(bf16)
        zb_ref[1, bx, by] = zi.astype(bf16)


def forward(pair, ar, ai, bt):
    _, _, nx, ny, _ = geometry()
    shape = (2, nx, ny, NR * SG // (nx * ny), SG)
    return pl.pallas_call(
        functools.partial(forward_kernel, nx, ny),
        out_shape=[jax.ShapeDtypeStruct(shape, f32), jax.ShapeDtypeStruct(shape, bf16)],
        in_specs=[VM] * 4,
        out_specs=[VM] * 2,
        compiler_params=pltpu.CompilerParams(vmem_limit_bytes=LIMIT),
        name="forward",
    )(pair, ar, ai, bt)


def decode(vis, rows_own):
    _, _, nx, ny, nz = geometry()
    x, h, y, z = position()
    base = ((x * ny + y) * nz + z) * rows_own
    cell = vis[0:1].astype(i32)
    sub = cell // (SG * SG)
    row = (sub // NC) * SG + (cell // SG) % SG - base
    row = jnp.where(sub % NC == h, row, -1)
    n = vis.shape[1]
    hot_row = lax.broadcasted_iota(i32, (rows_own, n), 0) == row
    hot_col = lax.broadcasted_iota(i32, (SG, n), 0) == cell % SG
    return hot_row, jnp.where(hot_col, 1.0, 0.0).astype(bf16)


def grid_kernel(rows_own, all_ref, o_ref, n_ref, acc):
    count = all_ref.shape[0]
    acc[...] = jnp.zeros_like(acc)

    def step(k, carry):
        vis = all_ref[k]
        hot_row, hot_col = decode(vis, rows_own)
        parts = []
        for q in (1, 2):
            val = vis[q : q + 1]
            high = val.astype(bf16).astype(f32)
            parts += [high, val - high]
        parts.append(jnp.ones_like(vis[0:1]))
        left = jnp.concatenate([jnp.where(hot_row, v, 0.0) for v in parts], 0).astype(bf16)
        acc[...] += lax.dot_general(left, hot_col, (((1,), (1,)), ((), ())), preferred_element_type=f32)
        return carry

    lax.fori_loop(0, count, step, 0)
    got = [acc[q * rows_own : (q + 1) * rows_own] for q in range(5)]
    o_ref[:, :SG] = got[0] + got[1]
    o_ref[:, SG:] = got[2] + got[3]
    n_ref[:, :SG] = got[4]
    n_ref[:, SG:] = got[4]


def gridding(vis_all, rows_own):
    shape = jax.ShapeDtypeStruct((rows_own, 2 * SG), f32)
    return pl.pallas_call(
        functools.partial(grid_kernel, rows_own),
        out_shape=[shape, shape],
        in_specs=[VM],
        out_specs=[VM, VM],
        scratch_shapes=[pltpu.VMEM((5 * rows_own, SG), f32)],
        compiler_params=pltpu.CompilerParams(vmem_limit_bytes=LIMIT),
        name="gridding",
    )(vis_all)


def degrid_kernel(rows_own, m_ref, all_ref, out_ref):
    count = all_ref.shape[0]
    m = m_ref[...]
    both = jnp.concatenate([m[:, :SG], m[:, SG:]], 0)
    high = both.astype(bf16)
    low = (both - high.astype(f32)).astype(bf16)

    def step(k, carry):
        hot_row, hot_col = decode(all_ref[k], rows_own)
        val = jnp.dot(high, hot_col, preferred_element_type=f32) + jnp.dot(low, hot_col, preferred_element_type=f32)
        re = jnp.sum(jnp.where(hot_row, val[:rows_own], 0.0), 0, keepdims=True)
        im = jnp.sum(jnp.where(hot_row, val[rows_own:], 0.0), 0, keepdims=True)
        out_ref[k] = jnp.concatenate([re, im], 0)
        return carry

    lax.fori_loop(0, count, step, 0)


def degrid(m, vis_all):
    count, _, nv = vis_all.shape
    return pl.pallas_call(
        functools.partial(degrid_kernel, m.shape[0]),
        out_shape=jax.ShapeDtypeStruct((count, 2, nv), f32),
        in_specs=[VM, VM],
        out_specs=VM,
        compiler_params=pltpu.CompilerParams(vmem_limit_bytes=LIMIT),
        name="degrid",
    )(m, vis_all)


def reduce_kernel(
    scale, z_ref, zb_ref, o_ref, n_ref, m_ref, g_ref,
    acc_a, acc_b, send_a, send_b, got_a1, got_b1, got_a2, got_b2,
    own_z, send_z, got_z, gz, ssem, rsem,
):
    _, _, nx, ny, nz = geometry()
    x, h, y, z = position()
    rows_own = m_ref.shape[0]

    def peer(dx, dy, dz):
        px = lax.rem(x + dx + nx, nx)
        py = lax.rem(y + dy + ny, ny)
        pz = lax.rem(z + dz + nz, nz)
        return (px * 2 + h, pz * ny + py), px, py, pz

    barrier = pltpu.get_barrier_semaphore()
    friends = (
        [(d, 0, 0) for d in range(1, nx)] + [(0, d, 0) for d in range(1, ny)] + [(0, 0, d) for d in range(1, nz)]
    )
    for dx, dy, dz in friends:
        pl.semaphore_signal(barrier, inc=1, device_id=peer(dx, dy, dz)[0], device_id_type=MESH)
    pl.semaphore_wait(barrier, len(friends))
    used = [0]

    def send(src, dst, to):
        k = used[0]
        used[0] += 1
        copy = pltpu.make_async_remote_copy(
            src, dst, ssem.at[k], rsem.at[k], device_id=to, device_id_type=MESH
        )
        copy.start()
        return copy, k

    def land(copies, dst=None):
        for t, (copy, k) in enumerate(copies):
            copy.wait_send()
            if dst is None:
                copy.wait_recv()
            else:
                pltpu.make_async_remote_copy(
                    dst[t], dst[t], ssem.at[k], rsem.at[k], device_id=peer(0, 0, 0)[0], device_id_type=MESH
                ).wait_recv()

    first_a, first_b = [], []
    for d in range(1, nx):
        to, px, _, _ = peer(d, 0, 0)
        first_a.append(send(zb_ref.at[0, px], got_a1.at[d - 1], to))
    for d in range(1, ny):
        to, _, py, _ = peer(0, d, 0)
        first_b.append(send(zb_ref.at[1, :, py], got_b1.at[d - 1], to))
    land(first_a)
    total = z_ref[0, x]
    for d in range(nx - 1):
        total = total + got_a1[d].astype(f32)
    acc_a[...] = total
    send_a[...] = total.astype(bf16)
    second_a, second_b = [], []
    for d in range(1, ny):
        to, _, py, _ = peer(0, d, 0)
        second_a.append(send(send_a.at[py], got_a2.at[d - 1], to))
    land(first_b)
    total = z_ref[1, :, y]
    for d in range(ny - 1):
        total = total + got_b1[d].astype(f32)
    acc_b[...] = total
    send_b[...] = total.astype(bf16)
    for d in range(1, nx):
        to, px, _, _ = peer(d, 0, 0)
        second_b.append(send(send_b.at[px], got_b2.at[d - 1], to))
    land(second_a)
    re = acc_a[y]
    for d in range(ny - 1):
        re = re + got_a2[d].astype(f32)
    land(second_b)
    im = acc_b[x]
    for d in range(nx - 1):
        im = im + got_b2[d].astype(f32)
    for k in range(nz):
        cut = slice(k * rows_own, (k + 1) * rows_own)
        own_z[k, :, :SG] = re[cut]
        own_z[k, :, SG:] = im[cut]
        send_z[k, :, :SG] = re[cut].astype(bf16)
        send_z[k, :, SG:] = im[cut].astype(bf16)
    third = []
    for d in range(1, nz):
        to, _, _, pz = peer(0, 0, d)
        third.append(send(send_z.at[pz], got_z.at[d - 1], to))
    land(third)
    total = own_z[z]
    for d in range(nz - 1):
        total = total + got_z[d].astype(f32)
    model = total * scale
    m_ref[...] = model
    gz[z] = (o_ref[...] - n_ref[...] * model).astype(bf16)
    fourth, dst = [], []
    for d in range(1, nz):
        to, _, _, _ = peer(0, 0, d)
        fourth.append(send(gz.at[z], gz.at[z], to))
        dst.append(gz.at[peer(0, 0, -d)[3]])
    land(fourth, dst)
    for k in range(nz):
        cut = slice(k * rows_own, (k + 1) * rows_own)
        g_ref[0, x, y, cut, :] = gz[k, :, :SG]
        g_ref[1, x, y, cut, :] = gz[k, :, SG:]
    fifth_a, fifth_b, dst_a, dst_b = [], [], [], []
    for d in range(1, ny):
        fifth_a.append(send(g_ref.at[0, x, y], g_ref.at[0, x, y], peer(0, d, 0)[0]))
        dst_a.append(g_ref.at[0, x, peer(0, -d, 0)[2]])
    for d in range(1, nx):
        fifth_b.append(send(g_ref.at[1, x, y], g_ref.at[1, x, y], peer(d, 0, 0)[0]))
        dst_b.append(g_ref.at[1, peer(-d, 0, 0)[1], y])
    land(fifth_a, dst_a)
    sixth_a, sixth_b, end_a, end_b = [], [], [], []
    for d in range(1, nx):
        sixth_a.append(send(g_ref.at[0, x], g_ref.at[0, x], peer(d, 0, 0)[0]))
        end_a.append(g_ref.at[0, peer(-d, 0, 0)[1]])
    land(fifth_b, dst_b)
    for d in range(1, ny):
        sixth_b.append(send(g_ref.at[1, :, y], g_ref.at[1, :, y], peer(0, d, 0)[0]))
        end_b.append(g_ref.at[1, :, peer(0, -d, 0)[2]])
    land(sixth_a, end_a)
    land(sixth_b, end_b)


def reduce_cycle(z, zb, o, n, scale):
    _, _, nx, ny, nz = geometry()
    rows_own = o.shape[0]
    long = nz * rows_own
    copies = 3 * (nx - 1) + 3 * (ny - 1) + 2 * (nz - 1) + (nx - 1) + (ny - 1)
    return pl.pallas_call(
        functools.partial(reduce_kernel, scale),
        out_shape=[jax.ShapeDtypeStruct(o.shape, f32), jax.ShapeDtypeStruct(zb.shape, bf16)],
        in_specs=[VM] * 4,
        out_specs=[VM] * 2,
        scratch_shapes=[
            pltpu.VMEM((ny, long, SG), f32),
            pltpu.VMEM((nx, long, SG), f32),
            pltpu.VMEM((ny, long, SG), bf16),
            pltpu.VMEM((nx, long, SG), bf16),
            pltpu.VMEM((nx - 1, ny, long, SG), bf16),
            pltpu.VMEM((ny - 1, nx, long, SG), bf16),
            pltpu.VMEM((ny - 1, long, SG), bf16),
            pltpu.VMEM((nx - 1, long, SG), bf16),
            pltpu.VMEM((nz, rows_own, 2 * SG), f32),
            pltpu.VMEM((nz, rows_own, 2 * SG), bf16),
            pltpu.VMEM((nz - 1, rows_own, 2 * SG), bf16),
            pltpu.VMEM((nz, rows_own, 2 * SG), bf16),
            pltpu.SemaphoreType.DMA((copies,)),
            pltpu.SemaphoreType.DMA((copies,)),
        ],
        compiler_params=pltpu.CompilerParams(
            collective_id=1, has_side_effects=True, vmem_limit_bytes=LIMIT
        ),
        name="cycle",
    )(z, zb, o, n)


def backward_kernel(scale, g_ref, ar_ref, ai_ref, bt_ref, own_ref, other_ref):
    x, h, y, z = position()
    fs = own_ref.shape[0]
    gr = g_ref[0]
    gi = g_ref[1]
    g = jnp.concatenate([gr, gi], 1)

    def rows(k):
        cut = pl.ds(pl.multiple_of(k * fs, fs), fs)
        first = (((0,), (0,)), ((), ()))
        one = lax.dot_general(ar_ref[:, cut], g, first, preferred_element_type=f32)
        two = lax.dot_general(ai_ref[:, cut], g, first, preferred_element_type=f32)
        u = jnp.concatenate([one[:, :SG] + two[:, SG:], one[:, SG:] - two[:, :SG]], 1).astype(bf16)
        return jnp.dot(u, bt_ref[...], preferred_element_type=f32) * scale

    other_ref[...] = rows(1 - h).astype(bf16)
    own_ref[...] = rows(h)


def backward(g, ar, ai, bt, scale):
    fs = bt.shape[1]
    return pl.pallas_call(
        functools.partial(backward_kernel, scale),
        out_shape=[jax.ShapeDtypeStruct((fs, fs), f32), jax.ShapeDtypeStruct((fs, fs), bf16)],
        in_specs=[VM] * 4,
        out_specs=[VM] * 2,
        compiler_params=pltpu.CompilerParams(vmem_limit_bytes=LIMIT),
        name="backward",
    )(g, ar, ai, bt)


def last_kernel(other_ref, vals_ref, got_ref, sums_ref, slots, lsem, ssem, rsem, vs, vr):
    rows, cols, _, _, _ = geometry()
    frow = lax.axis_index("frow")
    fcol = lax.axis_index("fcol")
    h = frow % 2
    n = rows * cols
    me = frow * cols + fcol
    greet_all(n, cols, me)
    sib = frow + 1 - 2 * h
    big = pltpu.make_async_remote_copy(
        other_ref, got_ref, ssem, rsem, device_id=(sib, fcol), device_id_type=MESH
    )
    big.start()

    def link(d, to, slot):
        return pltpu.make_async_remote_copy(
            vals_ref.at[to], slots.at[slot], vs.at[d], vr.at[d],
            device_id=(to // cols, to % cols), device_id_type=MESH,
        )

    everyone(n, cols, me, lambda d, to, frm: link(d, to, me).start())
    mine = pltpu.make_async_copy(vals_ref.at[me], slots.at[me], lsem)
    mine.start()
    mine.wait()
    everyone(n, cols, me, lambda d, to, frm: link(d, to, me).wait_send())
    everyone(n, cols, me, lambda d, to, frm: link(d, to, frm).wait_recv())
    sums_ref[...] = lax.fori_loop(1, n, lambda k, t: t + slots[k], slots[0])
    big.wait()


def last(other, vals):
    rows, cols, _, _, _ = geometry()
    n = rows * cols
    return pl.pallas_call(
        last_kernel,
        out_shape=[
            jax.ShapeDtypeStruct(other.shape, bf16),
            jax.ShapeDtypeStruct(vals.shape[1:], f32),
        ],
        in_specs=[VM, VM],
        out_specs=[VM, VM],
        scratch_shapes=[
            pltpu.VMEM(vals.shape, f32),
            pltpu.SemaphoreType.DMA,
            pltpu.SemaphoreType.DMA,
            pltpu.SemaphoreType.DMA,
            pltpu.SemaphoreType.DMA((n,)),
            pltpu.SemaphoreType.DMA((n,)),
        ],
        compiler_params=pltpu.CompilerParams(
            collective_id=2, has_side_effects=True, vmem_limit_bytes=LIMIT
        ),
        name="last",
    )(other, vals)


def shards(facet_image, row_offsets, col_offsets, vis_subgrid, vis_u, vis_v, observed):
    rows, cols, nx, ny, nz = geometry()
    fs = facet_image.shape[0]
    rows_own = NR * SG // (nx * ny * nz)
    scale_in = 1.0 / (fs * math.sqrt(rows * cols))
    scale_out = 1.0 / (SG * math.sqrt(NR * NC))
    cell = ((vis_subgrid * SG + vis_u) * SG + vis_v).astype(f32)
    vis = jnp.concatenate([cell[None], observed, jnp.zeros_like(cell)[None]], 0)
    pair, vis_all = swap(facet_image, vis)
    ar, ai, bt = tables(fs, row_offsets, col_offsets)
    z, zb = forward(pair, ar, ai, bt)
    o, n = gridding(vis_all, rows_own)
    m, g = reduce_cycle(z, zb, o, n, scale_in / SG)
    vals = degrid(m, vis_all)
    own, other = backward(g.reshape(2, NR * SG, SG), ar, ai, bt, scale_out / SG)
    got, sums = last(other, vals)
    return (own + got.astype(f32), observed - sums)


def solution(mesh):
    in_specs = (
        P("frow", "fcol"),
        P(),
        P(),
        P(("frow", "fcol")),
        P(("frow", "fcol")),
        P(("frow", "fcol")),
        P(None, ("frow", "fcol")),
    )
    out_specs = (P("frow", "fcol"), P(None, ("frow", "fcol")))
    return jax.shard_map(shards, mesh=mesh, in_specs=in_specs, out_specs=out_specs, check_vma=False)
```

```python
import functools
import math

import jax
import jax.numpy as jnp
from jax import lax
from jax.experimental import pallas as pl
from jax.experimental.pallas import tpu as pltpu
from jax.sharding import PartitionSpec as P

SKY = 65536
SG = 256
NR = 2
NC = 2
f32 = jnp.float32
bf16 = jnp.bfloat16
i32 = jnp.int32
MESH = pl.DeviceIdType.MESH
VM = pl.BlockSpec(memory_space=pltpu.VMEM)
SM = pl.BlockSpec(memory_space=pltpu.SMEM)
LIMIT = 60 << 20


def geometry():
    rows = lax.axis_size("frow")
    cols = lax.axis_size("fcol")
    nx = rows // 2
    ny = 1 << ((cols.bit_length() - 1) // 2)
    nz = cols // ny
    return rows, cols, nx, ny, nz


def position():
    _, _, _, ny, _ = geometry()
    frow = lax.axis_index("frow")
    fcol = lax.axis_index("fcol")
    return frow // 2, frow % 2, fcol % ny, fcol // ny


def dims(contract):
    return ((contract, contract), ((), ()))


def phase(product):
    angle = (product & (SKY - 1)).astype(f32) * (2.0 * math.pi / SKY)
    return jnp.cos(angle), jnp.sin(angle)


def expand(first, places, c_ref, s_ref):
    n = places.shape[1]
    steps = lax.broadcasted_iota(i32, (16, n), 0)
    c0, s0 = phase(steps * places)
    c1, s1 = phase((first + 16 * steps) * places)
    for k in range(SG // 16):
        ck = c1[k : k + 1]
        sk = s1[k : k + 1]
        c_ref[k * 16 : k * 16 + 16, :] = (ck * c0 - sk * s0).astype(bf16)
        s_ref[k * 16 : k * 16 + 16, :] = (sk * c0 + ck * s0).astype(bf16)


def place(q):
    _, _, _, ny, nz = geometry()
    return q // (ny * nz), (q // nz) % ny, q % nz


def device(q, h):
    _, _, _, ny, _ = geometry()
    x, y, z = place(q)
    return (2 * x + h, z * ny + y)


def hots(vis, h, base, rows_own):
    n = vis.shape[1]
    cell = vis[0:1].astype(i32)
    sub = cell // (SG * SG)
    row = (sub // NC) * SG + (cell // SG) % SG - base
    row = jnp.where(sub % NC == h, row, -1)
    hot_row = lax.broadcasted_iota(i32, (rows_own, n), 0) == row
    hot_col = lax.broadcasted_iota(i32, (SG, n), 0) == cell % SG
    return hot_row, jnp.where(hot_col, 1.0, 0.0).astype(bf16)


def main_kernel(
    scale, ro_ref, co_ref, sub_ref, u_ref, v_ref, obs_ref, facet_ref,
    g_ref, ar_ref, ai_ref, bt_ref, res_ref,
    kk, ks, rc, rs, vis_ref, vis_all, other, z_ref, zb_ref, grid_acc,
    acc_a, acc_b, send_a, send_b, got_a1, got_b1, got_a2, got_b2,
    own_z, send_z, got_z, gz, model, vals, pair_vals, slots,
    ssem, rsem, vs, vr, ws, wr, lsem,
):
    rows, cols, nx, ny, nz = geometry()
    x, h, y, z = position()
    chips = nx * ny * nz
    me = (x * ny + y) * nz + z
    fs = facet_ref.shape[0]
    nv = vis_ref.shape[1]
    rows_own = NR * SG // chips
    sib = (2 * x + 1 - h, lax.axis_index("fcol"))
    barrier = pltpu.get_barrier_semaphore()

    def peers(act):
        def step(d, carry):
            act(d, lax.rem(me + d, chips), lax.rem(me - d + chips, chips))
            return carry

        lax.fori_loop(1, chips, step, 0)

    peers(lambda d, to, frm: pl.semaphore_signal(barrier, inc=1, device_id=device(to, h), device_id_type=MESH))
    pl.semaphore_signal(barrier, inc=1, device_id=sib, device_id_type=MESH)
    cell = (sub_ref[...] * SG + u_ref[...]) * SG + v_ref[...]
    vis_ref[0:1] = cell.astype(f32)
    vis_ref[1:3] = obs_ref[...]
    vis_ref[3:4] = jnp.zeros((1, nv), f32)
    mine = pltpu.make_async_copy(vis_ref, vis_all.at[h, me], lsem)
    mine.start()
    expand(0, lax.broadcasted_iota(i32, (1, SG), 1) * (SKY // SG), kk, ks)
    pl.semaphore_wait(barrier, chips)
    used = [0]
    sent = []

    def send(src, dst, to):
        k = used[0]
        used[0] += 1
        copy = pltpu.make_async_remote_copy(
            src, dst, ssem.at[k], rsem.at[k], device_id=to, device_id_type=MESH
        )
        copy.start()
        sent.append(copy)
        return k

    def land(k, dst):
        pltpu.make_async_remote_copy(
            dst, dst, ssem.at[k], rsem.at[k], device_id=sib, device_id_type=MESH
        ).wait_recv()

    def link(d, to, slot):
        return pltpu.make_async_remote_copy(
            vis_ref, vis_all.at[h, slot], vs.at[d], vr.at[d],
            device_id=device(to, h), device_id_type=MESH,
        )

    k_facet = send(facet_ref, other, sib)
    peers(lambda d, to, frm: link(d, to, me).start())

    kcos = kk[...]
    ksin = ks[...]

    def compose(n):
        c = rc[:, :n]
        s = rs[:, :n]
        re = jnp.dot(kcos, c, preferred_element_type=f32) + jnp.dot(ksin, s, preferred_element_type=f32)
        im = jnp.dot(ksin, c, preferred_element_type=f32) - jnp.dot(kcos, s, preferred_element_type=f32)
        return re.astype(bf16), im.astype(bf16)

    step = SKY // (cols * fs)
    places = (lax.axis_index("fcol") * fs + lax.broadcasted_iota(i32, (1, fs), 1)) * step
    for c in range(NC):
        expand(co_ref[c], places, rc.at[:, :fs], rs.at[:, :fs])
        re, im = compose(fs)
        bt_ref[c, :SG] = re
        bt_ref[c, SG:] = im
    step = SKY // (rows * fs)
    places = (x * (2 * fs) + lax.broadcasted_iota(i32, (1, 2 * fs), 1)) * step
    for r in range(NR):
        expand(ro_ref[r], places, rc, rs)
        re, im = compose(2 * fs)
        ar_ref[r * SG : r * SG + SG] = re
        ai_ref[r * SG : r * SG + SG] = im

    mine.wait()
    bt = bt_ref[h]

    def project(ref):
        return lax.dot_general(ref[...], bt, (((1,), (1,)), ((), ())), preferred_element_type=f32).astype(bf16)

    own_p = project(facet_ref)
    peers(lambda d, to, frm: link(d, to, frm).wait_recv())
    k_vis = send(vis_all.at[h], vis_all.at[h], sib)
    land(k_facet, other)
    other_p = project(other)
    part = NR * SG // (nx * ny)
    own_cut = pl.ds(pl.multiple_of(h * fs, fs), fs)
    other_cut = pl.ds(pl.multiple_of((1 - h) * fs, fs), fs)
    first_a, first_b = [], []
    for dx in list(range(1, nx)) + [0]:
        px = lax.rem(x + dx, nx)
        for dy in list(range(1, ny)) + [0]:
            py = lax.rem(y + dy, ny)
            cut = pl.ds(pl.multiple_of((px * ny + py) * part, part), part)
            one = jnp.dot(ar_ref[cut, own_cut], own_p, preferred_element_type=f32)
            one += jnp.dot(ar_ref[cut, other_cut], other_p, preferred_element_type=f32)
            two = jnp.dot(ai_ref[cut, own_cut], own_p, preferred_element_type=f32)
            two += jnp.dot(ai_ref[cut, other_cut], other_p, preferred_element_type=f32)
            zr = one[:, :SG] - two[:, SG:]
            zi = one[:, SG:] + two[:, :SG]
            z_ref[0, px, py] = zr
            z_ref[1, px, py] = zi
            zb_ref[0, px, py] = zr.astype(bf16)
            zb_ref[1, px, py] = zi.astype(bf16)
            if dx == 0 and dy > 0:
                first_b.append(send(zb_ref.at[1, :, py], got_b1.at[dy - 1], device((x * ny + py) * nz + z, h)))
        if dx > 0:
            first_a.append(send(zb_ref.at[0, px], got_a1.at[dx - 1], device((px * ny + y) * nz + z, h)))

    base = me * rows_own
    grid_acc[...] = jnp.zeros_like(grid_acc)

    def gridding(side, lo, hi):
        def one(q):
            vis = vis_all[side, q]
            hot_row, hot_col = hots(vis, h, base, rows_own)
            parts = []
            for p in (1, 2):
                val = vis[p : p + 1]
                high = val.astype(bf16).astype(f32)
                parts += [high, val - high]
            parts.append(jnp.ones_like(vis[0:1]))
            left = jnp.concatenate([jnp.where(hot_row, t, 0.0) for t in parts], 0).astype(bf16)
            return lax.dot_general(left, hot_col, (((1,), (1,)), ((), ())), preferred_element_type=f32)

        def body(t, carry):
            got = one(lo + 2 * t) + one(lo + 2 * t + 1)
            grid_acc[...] += got
            return carry

        lax.fori_loop(0, (hi - lo) // 2, body, 0)

    half = chips // 2
    gridding(h, 0, half + half // 2)
    for k, dst in zip(first_a, range(nx - 1)):
        land(k, got_a1.at[dst])
    total = z_ref[0, x]
    for d in range(nx - 1):
        total = total + got_a1[d].astype(f32)
    acc_a[...] = total
    send_a[...] = total.astype(bf16)
    second_a, second_b = [], []
    for d in range(1, ny):
        py = lax.rem(y + d, ny)
        second_a.append(send(send_a.at[py], got_a2.at[d - 1], device((x * ny + py) * nz + z, h)))
    for k, dst in zip(first_b, range(ny - 1)):
        land(k, got_b1.at[dst])
    total = z_ref[1, :, y]
    for d in range(ny - 1):
        total = total + got_b1[d].astype(f32)
    acc_b[...] = total
    send_b[...] = total.astype(bf16)
    for d in range(1, nx):
        px = lax.rem(x + d, nx)
        second_b.append(send(send_b.at[px], got_b2.at[d - 1], device((px * ny + y) * nz + z, h)))
    gridding(h, half + half // 2, chips)
    land(k_vis, vis_all.at[1 - h])
    gridding(1 - h, 0, half // 2)
    for k, dst in zip(second_a, range(ny - 1)):
        land(k, got_a2.at[dst])
    re = acc_a[y]
    for d in range(ny - 1):
        re = re + got_a2[d].astype(f32)
    for k, dst in zip(second_b, range(nx - 1)):
        land(k, got_b2.at[dst])
    im = acc_b[x]
    for d in range(nx - 1):
        im = im + got_b2[d].astype(f32)
    for k in range(nz):
        cut = slice(k * rows_own, (k + 1) * rows_own)
        own_z[k, :, :SG] = re[cut]
        own_z[k, :, SG:] = im[cut]
        send_z[k, :, :SG] = re[cut].astype(bf16)
        send_z[k, :, SG:] = im[cut].astype(bf16)
    third = []
    for d in range(1, nz):
        pz = lax.rem(z + d, nz)
        third.append(send(send_z.at[pz], got_z.at[d - 1], device((x * ny + y) * nz + pz, h)))
    gridding(1 - h, half // 2, chips)
    for k, dst in zip(third, range(nz - 1)):
        land(k, got_z.at[dst])
    total = own_z[z]
    for d in range(nz - 1):
        total = total + got_z[d].astype(f32)
    m = total * scale
    got = [grid_acc[p * rows_own : (p + 1) * rows_own] for p in range(5)]
    hat_re = got[0] + got[1] - got[4] * m[:, :SG]
    hat_im = got[2] + got[3] - got[4] * m[:, SG:]
    gz[z, :, :SG] = hat_re.astype(bf16)
    gz[z, :, SG:] = hat_im.astype(bf16)
    fourth = []
    for d in range(1, nz):
        pz = lax.rem(z + d, nz)
        fourth.append(send(gz.at[z], gz.at[z], device((x * ny + y) * nz + pz, h)))
    both = jnp.concatenate([m[:, :SG], m[:, SG:]], 0)
    high = both.astype(bf16)
    model[: 2 * rows_own] = high
    model[2 * rows_own :] = (both - high.astype(f32)).astype(bf16)

    def degrid(side, lo, hi):
        def one(q):
            hot_row, hot_col = hots(vis_all[side, q], h, base, rows_own)
            val = jnp.dot(model[...], hot_col, preferred_element_type=f32)
            val = val[: 2 * rows_own] + val[2 * rows_own :]
            vr_ = jnp.sum(jnp.where(hot_row, val[:rows_own], 0.0), 0, keepdims=True)
            vi_ = jnp.sum(jnp.where(hot_row, val[rows_own:], 0.0), 0, keepdims=True)
            return jnp.concatenate([vr_, vi_], 0)

        def body(t, carry):
            a = one(lo + 2 * t)
            b = one(lo + 2 * t + 1)
            vals[side, lo + 2 * t] = a
            vals[side, lo + 2 * t + 1] = b
            return carry

        lax.fori_loop(0, (hi - lo) // 2, body, 0)

    degrid(1 - h, 0, chips)
    k_vals = send(vals.at[1 - h], pair_vals, sib)
    for k, d in zip(fourth, range(1, nz)):
        land(k, gz.at[lax.rem(z - d + nz, nz)])
    for k in range(nz):
        cut = slice(k * rows_own, (k + 1) * rows_own)
        g_ref[h, 0, x, y, cut, :] = gz[k, :, :SG]
        g_ref[h, 1, x, y, cut, :] = gz[k, :, SG:]
    fifth_a, fifth_b, cross = [], [], []

    def over(index):
        src = g_ref.at[(h,) + index]
        cross.append((send(src, src, sib), index))

    for d in range(1, ny):
        blk = g_ref.at[h, 0, x, y]
        fifth_a.append(send(blk, blk, device((x * ny + lax.rem(y + d, ny)) * nz + z, h)))
    for d in range(1, nx):
        blk = g_ref.at[h, 1, x, y]
        fifth_b.append(send(blk, blk, device((lax.rem(x + d, nx) * ny + y) * nz + z, h)))
    over((0, x, y))
    over((1, x, y))
    degrid(h, 0, half)
    for k, d in zip(fifth_a, range(1, ny)):
        land(k, g_ref.at[h, 0, x, lax.rem(y - d + ny, ny)])
    sixth_a, sixth_b = [], []
    for d in range(1, nx):
        blk = g_ref.at[h, 0, x]
        sixth_a.append(send(blk, blk, device((lax.rem(x + d, nx) * ny + y) * nz + z, h)))
    for k, d in zip(fifth_b, range(1, nx)):
        land(k, g_ref.at[h, 1, lax.rem(x - d + nx, nx), y])
    for d in range(1, ny):
        blk = g_ref.at[h, 1, :, y]
        sixth_b.append(send(blk, blk, device((x * ny + lax.rem(y + d, ny)) * nz + z, h)))
    for d in range(1, ny):
        over((0, x, lax.rem(y - d + ny, ny)))
    for d in range(1, nx):
        over((1, lax.rem(x - d + nx, nx), y))
    degrid(h, half, chips)
    land(k_vals, pair_vals)
    vals[h] = vals[h] + pair_vals[...]

    def back(d, to, slot):
        return pltpu.make_async_remote_copy(
            vals.at[h, to], slots.at[slot], ws.at[d], wr.at[d],
            device_id=device(to, h), device_id_type=MESH,
        )

    peers(lambda d, to, frm: back(d, to, me).start())
    for k, d in zip(sixth_a, range(1, nx)):
        px = lax.rem(x - d + nx, nx)
        land(k, g_ref.at[h, 0, px])
        over((0, px))
    for k, d in zip(sixth_b, range(1, ny)):
        py = lax.rem(y - d + ny, ny)
        land(k, g_ref.at[h, 1, :, py])
        over((1, slice(None), py))
    peers(lambda d, to, frm: back(d, to, frm).wait_recv())
    start = vals[h, me]
    res_ref[...] = obs_ref[...] - lax.fori_loop(
        1, chips, lambda d, t: t + slots[lax.rem(me + d, chips)], start
    )
    for k, index in cross:
        land(k, g_ref.at[(1 - h,) + index])
    for copy in sent:
        copy.wait_send()
    peers(lambda d, to, frm: link(d, to, me).wait_send())
    peers(lambda d, to, frm: back(d, to, me).wait_send())


def main(ro, co, sub, u, v, obs, facet, scale):
    _, _, nx, ny, nz = geometry()
    chips = nx * ny * nz
    fs = facet.shape[0]
    nv = obs.shape[1]
    rows_own = NR * SG // chips
    long = nz * rows_own
    copies = 64
    dma = pltpu.SemaphoreType.DMA
    return pl.pallas_call(
        functools.partial(main_kernel, scale),
        out_shape=[
            jax.ShapeDtypeStruct((2, 2, nx, ny, long, SG), bf16),
            jax.ShapeDtypeStruct((NR * SG, 2 * fs), bf16),
            jax.ShapeDtypeStruct((NR * SG, 2 * fs), bf16),
            jax.ShapeDtypeStruct((NC, 2 * SG, fs), bf16),
            jax.ShapeDtypeStruct((2, nv), f32),
        ],
        in_specs=[SM, SM] + [VM] * 5,
        out_specs=[VM] * 5,
        scratch_shapes=[
            pltpu.VMEM((SG, SG), bf16),
            pltpu.VMEM((SG, SG), bf16),
            pltpu.VMEM((SG, 2 * fs), bf16),
            pltpu.VMEM((SG, 2 * fs), bf16),
            pltpu.VMEM((4, nv), f32),
            pltpu.VMEM((2, chips, 4, nv), f32),
            pltpu.VMEM((fs, fs), bf16),
            pltpu.VMEM((2, nx, ny, long, SG), f32),
            pltpu.VMEM((2, nx, ny, long, SG), bf16),
            pltpu.VMEM((5 * rows_own, SG), f32),
            pltpu.VMEM((ny, long, SG), f32),
            pltpu.VMEM((nx, long, SG), f32),
            pltpu.VMEM((ny, long, SG), bf16),
            pltpu.VMEM((nx, long, SG), bf16),
            pltpu.VMEM((nx - 1, ny, long, SG), bf16),
            pltpu.VMEM((ny - 1, nx, long, SG), bf16),
            pltpu.VMEM((ny - 1, long, SG), bf16),
            pltpu.VMEM((nx - 1, long, SG), bf16),
            pltpu.VMEM((nz, rows_own, 2 * SG), f32),
            pltpu.VMEM((nz, rows_own, 2 * SG), bf16),
            pltpu.VMEM((nz - 1, rows_own, 2 * SG), bf16),
            pltpu.VMEM((nz, rows_own, 2 * SG), bf16),
            pltpu.VMEM((4 * rows_own, SG), bf16),
            pltpu.VMEM((2, chips, 2, nv), f32),
            pltpu.VMEM((chips, 2, nv), f32),
            pltpu.VMEM((chips, 2, nv), f32),
            dma((copies,)),
            dma((copies,)),
            dma((chips,)),
            dma((chips,)),
            dma((chips,)),
            dma((chips,)),
            dma,
        ],
        compiler_params=pltpu.CompilerParams(
            collective_id=0, has_side_effects=True, vmem_limit_bytes=LIMIT
        ),
        name="cycle",
    )(ro, co, sub, u, v, obs, facet)


def backward_kernel(scale, g_ref, ar_ref, ai_ref, bt_ref, image_ref):
    _, h, _, _ = position()
    fs = image_ref.shape[0]
    cut = pl.ds(pl.multiple_of(h * fs, fs), fs)
    first = (((0,), (0,)), ((), ()))
    g = jnp.concatenate([g_ref[c, p] for c in range(NC) for p in range(2)], 1)
    one = lax.dot_general(ar_ref[:, cut], g, first, preferred_element_type=f32)
    two = lax.dot_general(ai_ref[:, cut], g, first, preferred_element_type=f32)
    parts = []
    for c in range(NC):
        re = slice(2 * c * SG, (2 * c + 1) * SG)
        im = slice((2 * c + 1) * SG, (2 * c + 2) * SG)
        parts += [one[:, re] + two[:, im], one[:, im] - two[:, re]]
    u = jnp.concatenate(parts, 1).astype(bf16)
    b = bt_ref[...].reshape(2 * NC * SG, fs)
    image_ref[...] = jnp.dot(u, b, preferred_element_type=f32) * scale


def backward(g, ar, ai, bt, scale):
    fs = bt.shape[2]
    return pl.pallas_call(
        functools.partial(backward_kernel, scale),
        out_shape=jax.ShapeDtypeStruct((fs, fs), f32),
        in_specs=[VM] * 4,
        out_specs=VM,
        compiler_params=pltpu.CompilerParams(vmem_limit_bytes=LIMIT),
        name="backward",
    )(g, ar, ai, bt)


def shards(facet_image, row_offsets, col_offsets, vis_subgrid, vis_u, vis_v, observed):
    rows, cols, _, _, _ = geometry()
    fs = facet_image.shape[0]
    scale_in = 1.0 / (fs * math.sqrt(rows * cols))
    scale_out = 1.0 / (SG * math.sqrt(NR * NC))
    g, ar, ai, bt, residual = main(
        row_offsets, col_offsets, vis_subgrid[None], vis_u[None], vis_v[None],
        observed, facet_image, scale_in / SG,
    )
    image = backward(g.reshape(NC, 2, NR * SG, SG), ar, ai, bt, scale_out / SG)
    return (image, residual)


def solution(mesh):
    in_specs = (
        P("frow", "fcol"),
        P(),
        P(),
        P(("frow", "fcol")),
        P(("frow", "fcol")),
        P(("frow", "fcol")),
        P(None, ("frow", "fcol")),
    )
    out_specs = (P("frow", "fcol"), P(None, ("frow", "fcol")))
    return jax.shard_map(shards, mesh=mesh, in_specs=in_specs, out_specs=out_specs, check_vma=False)
```

```python
import functools
import math

import jax
import jax.numpy as jnp
from jax import lax
from jax.experimental import pallas as pl
from jax.experimental.pallas import tpu as pltpu
from jax.sharding import PartitionSpec as P

SKY = 65536
SG = 256
NR = 2
NC = 2
f32 = jnp.float32
bf16 = jnp.bfloat16
i32 = jnp.int32
MESH = pl.DeviceIdType.MESH
VM = pl.BlockSpec(memory_space=pltpu.VMEM)
SM = pl.BlockSpec(memory_space=pltpu.SMEM)
LIMIT = 60 << 20


def geometry():
    rows = lax.axis_size("frow")
    cols = lax.axis_size("fcol")
    nx = rows // 2
    ny = 1 << ((cols.bit_length() - 1) // 2)
    nz = cols // ny
    return rows, cols, nx, ny, nz


def position():
    _, _, _, ny, _ = geometry()
    frow = lax.axis_index("frow")
    fcol = lax.axis_index("fcol")
    return frow // 2, frow % 2, fcol % ny, fcol // ny


def dims(contract):
    return ((contract, contract), ((), ()))


def phase(product):
    angle = (product & (SKY - 1)).astype(f32) * (2.0 * math.pi / SKY)
    return jnp.cos(angle), jnp.sin(angle)


def expand(first, places, c_ref, s_ref):
    n = places.shape[1]
    steps = lax.broadcasted_iota(i32, (16, n), 0)
    c0, s0 = phase(steps * places)
    c1, s1 = phase((first + 16 * steps) * places)
    for k in range(SG // 16):
        ck = c1[k : k + 1]
        sk = s1[k : k + 1]
        c_ref[k * 16 : k * 16 + 16, :] = (ck * c0 - sk * s0).astype(bf16)
        s_ref[k * 16 : k * 16 + 16, :] = (sk * c0 + ck * s0).astype(bf16)


def place(q):
    _, _, _, ny, nz = geometry()
    return q // (ny * nz), (q // nz) % ny, q % nz


def device(q, h):
    _, _, _, ny, _ = geometry()
    x, y, z = place(q)
    return (2 * x + h, z * ny + y)


def hots(vis, h, base, rows_own):
    n = vis.shape[1]
    cell = vis[0:1].astype(i32)
    sub = cell // (SG * SG)
    row = (sub // NC) * SG + (cell // SG) % SG - base
    row = jnp.where(sub % NC == h, row, -1)
    hot_row = lax.broadcasted_iota(i32, (rows_own, n), 0) == row
    hot_col = lax.broadcasted_iota(i32, (SG, n), 0) == cell % SG
    return hot_row, jnp.where(hot_col, 1.0, 0.0).astype(bf16)


def main_kernel(
    scale, ro_ref, co_ref, sub_ref, u_ref, v_ref, obs_ref, facet_ref,
    g_ref, ar_ref, ai_ref, bt_ref, res_ref,
    kk, ks, rc, rs, vis_ref, vis_all, other, z_ref, zb_ref, grid_acc,
    acc_a, acc_b, send_a, send_b, got_a1, got_b1, got_a2, got_b2,
    own_z, send_z, got_z, gz, model, vals, pair_vals, slots,
    ssem, rsem, vs, vr, ws, wr, lsem,
):
    rows, cols, nx, ny, nz = geometry()
    x, h, y, z = position()
    chips = nx * ny * nz
    me = (x * ny + y) * nz + z
    fs = facet_ref.shape[0]
    nv = vis_ref.shape[1]
    rows_own = NR * SG // chips
    sib = (2 * x + 1 - h, lax.axis_index("fcol"))
    barrier = pltpu.get_barrier_semaphore()

    def peers(act):
        def step(d, carry):
            act(d, lax.rem(me + d, chips), lax.rem(me - d + chips, chips))
            return carry

        lax.fori_loop(1, chips, step, 0)

    peers(lambda d, to, frm: pl.semaphore_signal(barrier, inc=1, device_id=device(to, h), device_id_type=MESH))
    pl.semaphore_signal(barrier, inc=1, device_id=sib, device_id_type=MESH)
    cell = (sub_ref[...] * SG + u_ref[...]) * SG + v_ref[...]
    vis_ref[0:1] = cell.astype(f32)
    vis_ref[1:3] = obs_ref[...]
    vis_ref[3:4] = jnp.zeros((1, nv), f32)
    mine = pltpu.make_async_copy(vis_ref, vis_all.at[h, me], lsem)
    mine.start()
    expand(0, lax.broadcasted_iota(i32, (1, SG), 1) * (SKY // SG), kk, ks)
    pl.semaphore_wait(barrier, chips)
    used = [0]
    sent = []

    def send(src, dst, to):
        k = used[0]
        used[0] += 1
        copy = pltpu.make_async_remote_copy(
            src, dst, ssem.at[k], rsem.at[k], device_id=to, device_id_type=MESH
        )
        copy.start()
        sent.append(copy)
        return k

    def land(k, dst):
        pltpu.make_async_remote_copy(
            dst, dst, ssem.at[k], rsem.at[k], device_id=sib, device_id_type=MESH
        ).wait_recv()

    def link(d, to, slot):
        return pltpu.make_async_remote_copy(
            vis_ref, vis_all.at[h, slot], vs.at[d], vr.at[d],
            device_id=device(to, h), device_id_type=MESH,
        )

    k_facet = send(facet_ref, other, sib)
    peers(lambda d, to, frm: link(d, to, me).start())

    kcos = kk[...]
    ksin = ks[...]
    wide = SG // 2
    waves = range(2)

    def compose(n, start, unit):
        places = (start + lax.broadcasted_iota(i32, (1, n), 1)) * unit
        expand(0, places, rc.at[:, :n], rs.at[:, :n])
        c = rc[:, :n]
        s = rs[:, :n]
        re = jnp.dot(kcos, c, preferred_element_type=f32) + jnp.dot(ksin, s, preferred_element_type=f32)
        im = jnp.dot(ksin, c, preferred_element_type=f32) - jnp.dot(kcos, s, preferred_element_type=f32)

        def shifted(offset):
            cos, sin = phase(offset * places)
            return (re * cos + im * sin).astype(bf16), (im * cos - re * sin).astype(bf16)

        return shifted

    shifted = compose(fs, lax.axis_index("fcol") * fs, SKY // (cols * fs))
    for c in range(NC):
        bt_ref[c, :SG], bt_ref[c, SG:] = shifted(co_ref[c])
    shifted = compose(2 * fs, x * (2 * fs), SKY // (rows * fs))
    for r in range(NR):
        cut = slice(r * SG, r * SG + SG)
        ar_ref[cut], ai_ref[cut] = shifted(ro_ref[r])

    mine.wait()

    def project(ref, w):
        re = bt_ref[h, w * wide : (w + 1) * wide]
        im = bt_ref[h, SG + w * wide : SG + (w + 1) * wide]
        b = jnp.concatenate([re, im], 0)
        return lax.dot_general(ref[...], b, (((1,), (1,)), ((), ())), preferred_element_type=f32).astype(bf16)

    part = NR * SG // (nx * ny)
    own_cut = pl.ds(pl.multiple_of(h * fs, fs), fs)
    other_cut = pl.ds(pl.multiple_of((1 - h) * fs, fs), fs)
    first_a, first_b, second_a, second_b = [[], []], [[], []], [[], []], [[], []]
    third, fourth, fifth_a, fifth_b = [[], []], [[], []], [[], []], [[], []]
    sixth_a, sixth_b = [[], []], [[], []]

    def to_x(d):
        return device((lax.rem(x + d, nx) * ny + y) * nz + z, h)

    def to_y(d):
        return device((x * ny + lax.rem(y + d, ny)) * nz + z, h)

    def to_z(d):
        return device((x * ny + y) * nz + lax.rem(z + d, nz), h)

    for w in waves:
        own_p = project(facet_ref, w)
        if w == 0:
            land(k_facet, other)
        other_p = project(other, w)
        for dx in list(range(1, nx)) + [0]:
            px = lax.rem(x + dx, nx)
            for dy in list(range(1, ny)) + [0]:
                py = lax.rem(y + dy, ny)
                cut = pl.ds(pl.multiple_of((px * ny + py) * part, part), part)
                one = jnp.dot(ar_ref[cut, own_cut], own_p, preferred_element_type=f32)
                one += jnp.dot(ar_ref[cut, other_cut], other_p, preferred_element_type=f32)
                two = jnp.dot(ai_ref[cut, own_cut], own_p, preferred_element_type=f32)
                two += jnp.dot(ai_ref[cut, other_cut], other_p, preferred_element_type=f32)
                zr = one[:, :wide] - two[:, wide:]
                zi = one[:, wide:] + two[:, :wide]
                z_ref[w, 0, px, py] = zr
                z_ref[w, 1, px, py] = zi
                zb_ref[w, 0, px, py] = zr.astype(bf16)
                zb_ref[w, 1, px, py] = zi.astype(bf16)
                if dx == 0 and dy > 0:
                    first_b[w].append(send(zb_ref.at[w, 1, :, py], got_b1.at[w, dy - 1], to_y(dy)))
            if dx > 0:
                first_a[w].append(send(zb_ref.at[w, 0, px], got_a1.at[w, dx - 1], to_x(dx)))

    peers(lambda d, to, frm: link(d, to, frm).wait_recv())
    k_vis = send(vis_all.at[h], vis_all.at[h], sib)

    base = me * rows_own
    grid_acc[...] = jnp.zeros_like(grid_acc)

    def gridding(side, lo, hi):
        def one(q):
            vis = vis_all[side, q]
            hot_row, hot_col = hots(vis, h, base, rows_own)
            parts = []
            for p in (1, 2):
                val = vis[p : p + 1]
                high = val.astype(bf16).astype(f32)
                parts += [high, val - high]
            parts.append(jnp.ones_like(vis[0:1]))
            left = jnp.concatenate([jnp.where(hot_row, t, 0.0) for t in parts], 0).astype(bf16)
            return lax.dot_general(left, hot_col, (((1,), (1,)), ((), ())), preferred_element_type=f32)

        def body(t, carry):
            got = one(lo + 2 * t) + one(lo + 2 * t + 1)
            grid_acc[...] += got
            return carry

        lax.fori_loop(0, (hi - lo) // 2, body, 0)

    half = chips // 2

    def stage_two(w):
        for d in range(nx - 1):
            land(first_a[w][d], got_a1.at[w, d])
        total = z_ref[w, 0, x]
        for d in range(nx - 1):
            total = total + got_a1[w, d].astype(f32)
        acc_a[w] = total
        send_a[w] = total.astype(bf16)
        for d in range(1, ny):
            second_a[w].append(send(send_a.at[w, lax.rem(y + d, ny)], got_a2.at[w, d - 1], to_y(d)))
        for d in range(ny - 1):
            land(first_b[w][d], got_b1.at[w, d])
        total = z_ref[w, 1, :, y]
        for d in range(ny - 1):
            total = total + got_b1[w, d].astype(f32)
        acc_b[w] = total
        send_b[w] = total.astype(bf16)
        for d in range(1, nx):
            second_b[w].append(send(send_b.at[w, lax.rem(x + d, nx)], got_b2.at[w, d - 1], to_x(d)))

    def stage_three(w):
        for d in range(ny - 1):
            land(second_a[w][d], got_a2.at[w, d])
        re = acc_a[w, y]
        for d in range(ny - 1):
            re = re + got_a2[w, d].astype(f32)
        for d in range(nx - 1):
            land(second_b[w][d], got_b2.at[w, d])
        im = acc_b[w, x]
        for d in range(nx - 1):
            im = im + got_b2[w, d].astype(f32)
        for k in range(nz):
            cut = slice(k * rows_own, (k + 1) * rows_own)
            own_z[w, k, :, :wide] = re[cut]
            own_z[w, k, :, wide:] = im[cut]
            send_z[w, k, :, :wide] = re[cut].astype(bf16)
            send_z[w, k, :, wide:] = im[cut].astype(bf16)
        for d in range(1, nz):
            third[w].append(send(send_z.at[w, lax.rem(z + d, nz)], got_z.at[w, d - 1], to_z(d)))

    def turn(w):
        for d in range(nz - 1):
            land(third[w][d], got_z.at[w, d])
        total = own_z[w, z]
        for d in range(nz - 1):
            total = total + got_z[w, d].astype(f32)
        m = total * scale
        cut = slice(w * wide, (w + 1) * wide)
        got = [grid_acc[p * rows_own : (p + 1) * rows_own, cut] for p in range(5)]
        hat_re = got[0] + got[1] - got[4] * m[:, :wide]
        hat_im = got[2] + got[3] - got[4] * m[:, wide:]
        gz[w, z, :, :wide] = hat_re.astype(bf16)
        gz[w, z, :, wide:] = hat_im.astype(bf16)
        for d in range(1, nz):
            fourth[w].append(send(gz.at[w, z], gz.at[w, z], to_z(d)))
        both = jnp.concatenate([m[:, :wide], m[:, wide:]], 0)
        high = both.astype(bf16)
        model[: 2 * rows_own, cut] = high
        model[2 * rows_own :, cut] = (both - high.astype(f32)).astype(bf16)

    cross = []

    def over(index):
        src = g_ref.at[(h,) + index]
        cross.append((send(src, src, sib), index))

    def stage_five(w):
        for d in range(1, nz):
            land(fourth[w][d - 1], gz.at[w, lax.rem(z - d + nz, nz)])
        for k in range(nz):
            cut = slice(k * rows_own, (k + 1) * rows_own)
            g_ref[h, w, 0, x, y, cut, :] = gz[w, k, :, :wide]
            g_ref[h, w, 1, x, y, cut, :] = gz[w, k, :, wide:]
        for d in range(1, ny):
            blk = g_ref.at[h, w, 0, x, y]
            fifth_a[w].append(send(blk, blk, to_y(d)))
        for d in range(1, nx):
            blk = g_ref.at[h, w, 1, x, y]
            fifth_b[w].append(send(blk, blk, to_x(d)))
        over((w, 0, x, y))
        over((w, 1, x, y))

    def stage_six(w):
        for d in range(1, ny):
            land(fifth_a[w][d - 1], g_ref.at[h, w, 0, x, lax.rem(y - d + ny, ny)])
        for d in range(1, nx):
            blk = g_ref.at[h, w, 0, x]
            sixth_a[w].append(send(blk, blk, to_x(d)))
        for d in range(1, nx):
            land(fifth_b[w][d - 1], g_ref.at[h, w, 1, lax.rem(x - d + nx, nx), y])
        for d in range(1, ny):
            blk = g_ref.at[h, w, 1, :, y]
            sixth_b[w].append(send(blk, blk, to_y(d)))
        for d in range(1, ny):
            over((w, 0, x, lax.rem(y - d + ny, ny)))
        for d in range(1, nx):
            over((w, 1, lax.rem(x - d + nx, nx), y))

    def finish(w):
        for d in range(1, nx):
            px = lax.rem(x - d + nx, nx)
            land(sixth_a[w][d - 1], g_ref.at[h, w, 0, px])
            over((w, 0, px))
        for d in range(1, ny):
            py = lax.rem(y - d + ny, ny)
            land(sixth_b[w][d - 1], g_ref.at[h, w, 1, :, py])
            over((w, 1, slice(None), py))

    def degrid(side, lo, hi):
        def one(q):
            hot_row, hot_col = hots(vis_all[side, q], h, base, rows_own)
            val = jnp.dot(model[...], hot_col, preferred_element_type=f32)
            val = val[: 2 * rows_own] + val[2 * rows_own :]
            vr_ = jnp.sum(jnp.where(hot_row, val[:rows_own], 0.0), 0, keepdims=True)
            vi_ = jnp.sum(jnp.where(hot_row, val[rows_own:], 0.0), 0, keepdims=True)
            return jnp.concatenate([vr_, vi_], 0)

        def body(t, carry):
            a = one(lo + 2 * t)
            b = one(lo + 2 * t + 1)
            vals[side, lo + 2 * t] = a
            vals[side, lo + 2 * t + 1] = b
            return carry

        lax.fori_loop(0, (hi - lo) // 2, body, 0)

    def back(d, to, slot):
        return pltpu.make_async_remote_copy(
            vals.at[h, to], slots.at[slot], ws.at[d], wr.at[d],
            device_id=device(to, h), device_id_type=MESH,
        )

    stage_two(0)
    gridding(h, 0, half)
    stage_two(1)
    gridding(h, half, chips)
    stage_three(0)
    land(k_vis, vis_all.at[1 - h])
    gridding(1 - h, 0, half)
    stage_three(1)
    gridding(1 - h, half, chips)
    turn(0)
    turn(1)
    degrid(1 - h, 0, half)
    stage_five(0)
    degrid(1 - h, half, chips)
    k_vals = send(vals.at[1 - h], pair_vals, sib)
    stage_five(1)
    degrid(h, 0, half)
    stage_six(0)
    degrid(h, half, chips)
    stage_six(1)
    land(k_vals, pair_vals)
    vals[h] = vals[h] + pair_vals[...]
    peers(lambda d, to, frm: back(d, to, me).start())
    finish(0)
    finish(1)
    peers(lambda d, to, frm: back(d, to, frm).wait_recv())
    start = vals[h, me]
    res_ref[...] = obs_ref[...] - lax.fori_loop(
        1, chips, lambda d, t: t + slots[lax.rem(me + d, chips)], start
    )
    for k, index in cross:
        land(k, g_ref.at[(1 - h,) + index])
    for copy in sent:
        copy.wait_send()
    peers(lambda d, to, frm: link(d, to, me).wait_send())
    peers(lambda d, to, frm: back(d, to, me).wait_send())


def main(ro, co, sub, u, v, obs, facet, scale):
    _, _, nx, ny, nz = geometry()
    chips = nx * ny * nz
    fs = facet.shape[0]
    nv = obs.shape[1]
    rows_own = NR * SG // chips
    long = nz * rows_own
    copies = 128
    dma = pltpu.SemaphoreType.DMA
    return pl.pallas_call(
        functools.partial(main_kernel, scale),
        out_shape=[
            jax.ShapeDtypeStruct((2, 2, 2, nx, ny, long, SG // 2), bf16),
            jax.ShapeDtypeStruct((NR * SG, 2 * fs), bf16),
            jax.ShapeDtypeStruct((NR * SG, 2 * fs), bf16),
            jax.ShapeDtypeStruct((NC, 2 * SG, fs), bf16),
            jax.ShapeDtypeStruct((2, nv), f32),
        ],
        in_specs=[SM, SM] + [VM] * 5,
        out_specs=[VM] * 5,
        scratch_shapes=[
            pltpu.VMEM((SG, SG), bf16),
            pltpu.VMEM((SG, SG), bf16),
            pltpu.VMEM((SG, 2 * fs), bf16),
            pltpu.VMEM((SG, 2 * fs), bf16),
            pltpu.VMEM((4, nv), f32),
            pltpu.VMEM((2, chips, 4, nv), f32),
            pltpu.VMEM((fs, fs), bf16),
            pltpu.VMEM((2, 2, nx, ny, long, SG // 2), f32),
            pltpu.VMEM((2, 2, nx, ny, long, SG // 2), bf16),
            pltpu.VMEM((5 * rows_own, SG), f32),
            pltpu.VMEM((2, ny, long, SG // 2), f32),
            pltpu.VMEM((2, nx, long, SG // 2), f32),
            pltpu.VMEM((2, ny, long, SG // 2), bf16),
            pltpu.VMEM((2, nx, long, SG // 2), bf16),
            pltpu.VMEM((2, nx - 1, ny, long, SG // 2), bf16),
            pltpu.VMEM((2, ny - 1, nx, long, SG // 2), bf16),
            pltpu.VMEM((2, ny - 1, long, SG // 2), bf16),
            pltpu.VMEM((2, nx - 1, long, SG // 2), bf16),
            pltpu.VMEM((2, nz, rows_own, SG), f32),
            pltpu.VMEM((2, nz, rows_own, SG), bf16),
            pltpu.VMEM((2, nz - 1, rows_own, SG), bf16),
            pltpu.VMEM((2, nz, rows_own, SG), bf16),
            pltpu.VMEM((4 * rows_own, SG), bf16),
            pltpu.VMEM((2, chips, 2, nv), f32),
            pltpu.VMEM((chips, 2, nv), f32),
            pltpu.VMEM((chips, 2, nv), f32),
            dma((copies,)),
            dma((copies,)),
            dma((chips,)),
            dma((chips,)),
            dma((chips,)),
            dma((chips,)),
            dma,
        ],
        compiler_params=pltpu.CompilerParams(
            collective_id=0, has_side_effects=True, vmem_limit_bytes=LIMIT
        ),
        name="cycle",
    )(ro, co, sub, u, v, obs, facet)


def backward_kernel(scale, g_ref, ar_ref, ai_ref, bt_ref, image_ref):
    _, h, _, _ = position()
    fs = image_ref.shape[0]
    cut = pl.ds(pl.multiple_of(h * fs, fs), fs)
    first = (((0,), (0,)), ((), ()))
    g = jnp.concatenate([g_ref[c, w, p] for c in range(NC) for p in range(2) for w in range(2)], 1)
    one = lax.dot_general(ar_ref[:, cut], g, first, preferred_element_type=f32)
    two = lax.dot_general(ai_ref[:, cut], g, first, preferred_element_type=f32)
    parts = []
    for c in range(NC):
        re = slice(2 * c * SG, (2 * c + 1) * SG)
        im = slice((2 * c + 1) * SG, (2 * c + 2) * SG)
        parts += [one[:, re] + two[:, im], one[:, im] - two[:, re]]
    u = jnp.concatenate(parts, 1).astype(bf16)
    b = bt_ref[...].reshape(2 * NC * SG, fs)
    image_ref[...] = jnp.dot(u, b, preferred_element_type=f32) * scale


def backward(g, ar, ai, bt, scale):
    fs = bt.shape[2]
    return pl.pallas_call(
        functools.partial(backward_kernel, scale),
        out_shape=jax.ShapeDtypeStruct((fs, fs), f32),
        in_specs=[VM] * 4,
        out_specs=VM,
        compiler_params=pltpu.CompilerParams(vmem_limit_bytes=LIMIT),
        name="backward",
    )(g, ar, ai, bt)


def shards(facet_image, row_offsets, col_offsets, vis_subgrid, vis_u, vis_v, observed):
    rows, cols, _, _, _ = geometry()
    fs = facet_image.shape[0]
    scale_in = 1.0 / (fs * math.sqrt(rows * cols))
    scale_out = 1.0 / (SG * math.sqrt(NR * NC))
    g, ar, ai, bt, residual = main(
        row_offsets, col_offsets, vis_subgrid[None], vis_u[None], vis_v[None],
        observed, facet_image, scale_in / SG,
    )
    image = backward(g.reshape(NC, 2, 2, NR * SG, SG // 2), ar, ai, bt, scale_out / SG)
    return (image, residual)


def solution(mesh):
    in_specs = (
        P("frow", "fcol"),
        P(),
        P(),
        P(("frow", "fcol")),
        P(("frow", "fcol")),
        P(("frow", "fcol")),
        P(None, ("frow", "fcol")),
    )
    out_specs = (P("frow", "fcol"), P(None, ("frow", "fcol")))
    return jax.shard_map(shards, mesh=mesh, in_specs=in_specs, out_specs=out_specs, check_vma=False)
```

```python
import functools
import math

import jax
import jax.numpy as jnp
from jax import lax
from jax.experimental import pallas as pl
from jax.experimental.pallas import tpu as pltpu
from jax.sharding import PartitionSpec as P

SKY = 65536
SG = 256
NR = 2
NC = 2
f32 = jnp.float32
bf16 = jnp.bfloat16
i32 = jnp.int32
MESH = pl.DeviceIdType.MESH
VM = pl.BlockSpec(memory_space=pltpu.VMEM)
SM = pl.BlockSpec(memory_space=pltpu.SMEM)
LIMIT = 60 << 20


def geometry():
    rows = lax.axis_size("frow")
    cols = lax.axis_size("fcol")
    nx = rows // 2
    ny = 1 << ((cols.bit_length() - 1) // 2)
    nz = cols // ny
    return rows, cols, nx, ny, nz


def position():
    _, _, _, ny, _ = geometry()
    frow = lax.axis_index("frow")
    fcol = lax.axis_index("fcol")
    return frow // 2, frow % 2, fcol % ny, fcol // ny


def dims(contract):
    return ((contract, contract), ((), ()))


def phase(product):
    angle = (product & (SKY - 1)).astype(f32) * (2.0 * math.pi / SKY)
    return jnp.cos(angle), jnp.sin(angle)


def expand(first, places, c_ref, s_ref):
    n = places.shape[1]
    steps = lax.broadcasted_iota(i32, (16, n), 0)
    c0, s0 = phase(steps * places)
    c1, s1 = phase((first + 16 * steps) * places)
    for k in range(SG // 16):
        ck = c1[k : k + 1]
        sk = s1[k : k + 1]
        c_ref[k * 16 : k * 16 + 16, :] = (ck * c0 - sk * s0).astype(bf16)
        s_ref[k * 16 : k * 16 + 16, :] = (sk * c0 + ck * s0).astype(bf16)


def place(q):
    _, _, _, ny, nz = geometry()
    return q // (ny * nz), (q // nz) % ny, q % nz


def device(q, h):
    _, _, _, ny, _ = geometry()
    x, y, z = place(q)
    return (2 * x + h, z * ny + y)


def hots(vis, h, base, rows_own):
    n = vis.shape[1]
    cell = vis[0:1].astype(i32)
    sub = cell // (SG * SG)
    row = (sub // NC) * SG + (cell // SG) % SG - base
    row = jnp.where(sub % NC == h, row, -1)
    hot_row = lax.broadcasted_iota(i32, (rows_own, n), 0) == row
    hot_col = lax.broadcasted_iota(i32, (SG, n), 0) == cell % SG
    return hot_row, jnp.where(hot_col, 1.0, 0.0).astype(bf16)


def main_kernel(
    scale, ro_ref, co_ref, sub_ref, u_ref, v_ref, obs_ref, facet_ref,
    g_ref, ar_ref, ai_ref, bt_ref, res_ref,
    kk, ks, rc, rs, vis_ref, vis_all, other, z_ref, zb_ref, grid_acc,
    acc_a, acc_b, send_a, send_b, got_a1, got_b1, got_a2, got_b2,
    own_z, send_z, got_z, gz, model, vals, pair_vals, slots,
    ssem, rsem, vs, vr, ws, wr, lsem,
):
    rows, cols, nx, ny, nz = geometry()
    x, h, y, z = position()
    chips = nx * ny * nz
    me = (x * ny + y) * nz + z
    fs = facet_ref.shape[0]
    nv = vis_ref.shape[1]
    rows_own = NR * SG // chips
    sib = (2 * x + 1 - h, lax.axis_index("fcol"))
    barrier = pltpu.get_barrier_semaphore()

    def peers(act):
        def step(d, carry):
            act(d, lax.rem(me + d, chips), lax.rem(me - d + chips, chips))
            return carry

        lax.fori_loop(1, chips, step, 0)

    peers(lambda d, to, frm: pl.semaphore_signal(barrier, inc=1, device_id=device(to, h), device_id_type=MESH))
    pl.semaphore_signal(barrier, inc=1, device_id=sib, device_id_type=MESH)
    cell = (sub_ref[...] * SG + u_ref[...]) * SG + v_ref[...]
    vis_ref[0:1] = cell.astype(f32)
    vis_ref[1:3] = obs_ref[...]
    vis_ref[3:4] = jnp.zeros((1, nv), f32)
    mine = pltpu.make_async_copy(vis_ref, vis_all.at[h, me], lsem)
    mine.start()
    expand(0, lax.broadcasted_iota(i32, (1, SG), 1) * (SKY // SG), kk, ks)
    used = [0]
    sent = []

    def send(src, dst, to):
        k = used[0]
        used[0] += 1
        copy = pltpu.make_async_remote_copy(
            src, dst, ssem.at[k], rsem.at[k], device_id=to, device_id_type=MESH
        )
        copy.start()
        sent.append(copy)
        return k

    def land(k, dst):
        pltpu.make_async_remote_copy(
            dst, dst, ssem.at[k], rsem.at[k], device_id=sib, device_id_type=MESH
        ).wait_recv()

    def link(d, to, slot):
        return pltpu.make_async_remote_copy(
            vis_ref, vis_all.at[h, slot], vs.at[d], vr.at[d],
            device_id=device(to, h), device_id_type=MESH,
        )


    kcos = kk[...]
    ksin = ks[...]
    wide = SG // 2
    waves = range(2)

    def compose(n, start, unit):
        places = (start + lax.broadcasted_iota(i32, (1, n), 1)) * unit
        expand(0, places, rc.at[:, :n], rs.at[:, :n])
        c = rc[:, :n]
        s = rs[:, :n]
        re = jnp.dot(kcos, c, preferred_element_type=f32) + jnp.dot(ksin, s, preferred_element_type=f32)
        im = jnp.dot(ksin, c, preferred_element_type=f32) - jnp.dot(kcos, s, preferred_element_type=f32)

        def shifted(offset):
            cos, sin = phase(offset * places)
            return (re * cos + im * sin).astype(bf16), (im * cos - re * sin).astype(bf16)

        return shifted

    shifted = compose(fs, lax.axis_index("fcol") * fs, SKY // (cols * fs))
    for c in range(NC):
        bt_ref[c, :SG], bt_ref[c, SG:] = shifted(co_ref[c])
    pl.semaphore_wait(barrier, chips)
    k_facet = send(facet_ref, other, sib)
    peers(lambda d, to, frm: link(d, to, me).start())
    shifted = compose(2 * fs, x * (2 * fs), SKY // (rows * fs))
    for r in range(NR):
        cut = slice(r * SG, r * SG + SG)
        ar_ref[cut], ai_ref[cut] = shifted(ro_ref[r])

    mine.wait()

    def project(ref, w):
        re = bt_ref[h, w * wide : (w + 1) * wide]
        im = bt_ref[h, SG + w * wide : SG + (w + 1) * wide]
        b = jnp.concatenate([re, im], 0)
        return lax.dot_general(ref[...], b, (((1,), (1,)), ((), ())), preferred_element_type=f32).astype(bf16)

    part = NR * SG // (nx * ny)
    own_cut = pl.ds(pl.multiple_of(h * fs, fs), fs)
    other_cut = pl.ds(pl.multiple_of((1 - h) * fs, fs), fs)
    first_a, first_b, second_a, second_b = [[], []], [[], []], [[], []], [[], []]
    third, fourth, fifth_a, fifth_b = [[], []], [[], []], [[], []], [[], []]
    sixth_a, sixth_b = [[], []], [[], []]

    def to_x(d):
        return device((lax.rem(x + d, nx) * ny + y) * nz + z, h)

    def to_y(d):
        return device((x * ny + lax.rem(y + d, ny)) * nz + z, h)

    def to_z(d):
        return device((x * ny + y) * nz + lax.rem(z + d, nz), h)

    for w in waves:
        own_p = project(facet_ref, w)
        if w == 0:
            land(k_facet, other)
        other_p = project(other, w)
        for dx in list(range(1, nx)) + [0]:
            px = lax.rem(x + dx, nx)
            for dy in list(range(1, ny)) + [0]:
                py = lax.rem(y + dy, ny)
                cut = pl.ds(pl.multiple_of((px * ny + py) * part, part), part)
                one = jnp.dot(ar_ref[cut, own_cut], own_p, preferred_element_type=f32)
                one += jnp.dot(ar_ref[cut, other_cut], other_p, preferred_element_type=f32)
                two = jnp.dot(ai_ref[cut, own_cut], own_p, preferred_element_type=f32)
                two += jnp.dot(ai_ref[cut, other_cut], other_p, preferred_element_type=f32)
                zr = one[:, :wide] - two[:, wide:]
                zi = one[:, wide:] + two[:, :wide]
                z_ref[w, 0, px, py] = zr
                z_ref[w, 1, px, py] = zi
                zb_ref[w, 0, px, py] = zr.astype(bf16)
                zb_ref[w, 1, px, py] = zi.astype(bf16)
                if dx == 0 and dy > 0:
                    first_b[w].append(send(zb_ref.at[w, 1, :, py], got_b1.at[w, dy - 1], to_y(dy)))
            if dx > 0:
                first_a[w].append(send(zb_ref.at[w, 0, px], got_a1.at[w, dx - 1], to_x(dx)))

    peers(lambda d, to, frm: link(d, to, frm).wait_recv())
    k_vis = send(vis_all.at[h], vis_all.at[h], sib)

    base = me * rows_own
    grid_acc[...] = jnp.zeros_like(grid_acc)

    def gridding(side, lo, hi):
        def one(q):
            vis = vis_all[side, q]
            hot_row, hot_col = hots(vis, h, base, rows_own)
            parts = []
            for p in (1, 2):
                val = vis[p : p + 1]
                high = val.astype(bf16).astype(f32)
                parts += [high, val - high]
            parts.append(jnp.ones_like(vis[0:1]))
            left = jnp.concatenate([jnp.where(hot_row, t, 0.0) for t in parts], 0).astype(bf16)
            return lax.dot_general(left, hot_col, (((1,), (1,)), ((), ())), preferred_element_type=f32)

        def body(t, carry):
            got = one(lo + 2 * t) + one(lo + 2 * t + 1)
            grid_acc[...] += got
            return carry

        lax.fori_loop(0, (hi - lo) // 2, body, 0)

    half = chips // 2

    def stage_two(w):
        for d in range(nx - 1):
            land(first_a[w][d], got_a1.at[w, d])
        total = z_ref[w, 0, x]
        for d in range(nx - 1):
            total = total + got_a1[w, d].astype(f32)
        acc_a[w] = total
        send_a[w] = total.astype(bf16)
        for d in range(1, ny):
            second_a[w].append(send(send_a.at[w, lax.rem(y + d, ny)], got_a2.at[w, d - 1], to_y(d)))
        for d in range(ny - 1):
            land(first_b[w][d], got_b1.at[w, d])
        total = z_ref[w, 1, :, y]
        for d in range(ny - 1):
            total = total + got_b1[w, d].astype(f32)
        acc_b[w] = total
        send_b[w] = total.astype(bf16)
        for d in range(1, nx):
            second_b[w].append(send(send_b.at[w, lax.rem(x + d, nx)], got_b2.at[w, d - 1], to_x(d)))

    def stage_three(w):
        for d in range(ny - 1):
            land(second_a[w][d], got_a2.at[w, d])
        re = acc_a[w, y]
        for d in range(ny - 1):
            re = re + got_a2[w, d].astype(f32)
        for d in range(nx - 1):
            land(second_b[w][d], got_b2.at[w, d])
        im = acc_b[w, x]
        for d in range(nx - 1):
            im = im + got_b2[w, d].astype(f32)
        for k in range(nz):
            cut = slice(k * rows_own, (k + 1) * rows_own)
            own_z[w, k, :, :wide] = re[cut]
            own_z[w, k, :, wide:] = im[cut]
            send_z[w, k, :, :wide] = re[cut].astype(bf16)
            send_z[w, k, :, wide:] = im[cut].astype(bf16)
        for d in range(1, nz):
            third[w].append(send(send_z.at[w, lax.rem(z + d, nz)], got_z.at[w, d - 1], to_z(d)))

    def turn(w):
        for d in range(nz - 1):
            land(third[w][d], got_z.at[w, d])
        total = own_z[w, z]
        for d in range(nz - 1):
            total = total + got_z[w, d].astype(f32)
        m = total * scale
        cut = slice(w * wide, (w + 1) * wide)
        got = [grid_acc[p * rows_own : (p + 1) * rows_own, cut] for p in range(5)]
        hat_re = got[0] + got[1] - got[4] * m[:, :wide]
        hat_im = got[2] + got[3] - got[4] * m[:, wide:]
        gz[w, z, :, :wide] = hat_re.astype(bf16)
        gz[w, z, :, wide:] = hat_im.astype(bf16)
        for d in range(1, nz):
            fourth[w].append(send(gz.at[w, z], gz.at[w, z], to_z(d)))
        both = jnp.concatenate([m[:, :wide], m[:, wide:]], 0)
        high = both.astype(bf16)
        model[: 2 * rows_own, cut] = high
        model[2 * rows_own :, cut] = (both - high.astype(f32)).astype(bf16)

    cross = []

    def over(index):
        src = g_ref.at[(h,) + index]
        cross.append((send(src, src, sib), index))

    def stage_five(w):
        for d in range(1, nz):
            land(fourth[w][d - 1], gz.at[w, lax.rem(z - d + nz, nz)])
        for k in range(nz):
            cut = slice(k * rows_own, (k + 1) * rows_own)
            g_ref[h, w, 0, x, y, cut, :] = gz[w, k, :, :wide]
            g_ref[h, w, 1, x, y, cut, :] = gz[w, k, :, wide:]
        for d in range(1, ny):
            blk = g_ref.at[h, w, 0, x, y]
            fifth_a[w].append(send(blk, blk, to_y(d)))
        for d in range(1, nx):
            blk = g_ref.at[h, w, 1, x, y]
            fifth_b[w].append(send(blk, blk, to_x(d)))
        over((w, 0, x, y))
        over((w, 1, x, y))

    def stage_six(w):
        for d in range(1, ny):
            land(fifth_a[w][d - 1], g_ref.at[h, w, 0, x, lax.rem(y - d + ny, ny)])
        for d in range(1, nx):
            blk = g_ref.at[h, w, 0, x]
            sixth_a[w].append(send(blk, blk, to_x(d)))
        for d in range(1, nx):
            land(fifth_b[w][d - 1], g_ref.at[h, w, 1, lax.rem(x - d + nx, nx), y])
        for d in range(1, ny):
            blk = g_ref.at[h, w, 1, :, y]
            sixth_b[w].append(send(blk, blk, to_y(d)))
        for d in range(1, ny):
            over((w, 0, x, lax.rem(y - d + ny, ny)))
        for d in range(1, nx):
            over((w, 1, lax.rem(x - d + nx, nx), y))

    def finish(w):
        for d in range(1, nx):
            px = lax.rem(x - d + nx, nx)
            land(sixth_a[w][d - 1], g_ref.at[h, w, 0, px])
            over((w, 0, px))
        for d in range(1, ny):
            py = lax.rem(y - d + ny, ny)
            land(sixth_b[w][d - 1], g_ref.at[h, w, 1, :, py])
            over((w, 1, slice(None), py))

    def degrid(side, lo, hi):
        def one(q):
            hot_row, hot_col = hots(vis_all[side, q], h, base, rows_own)
            val = jnp.dot(model[...], hot_col, preferred_element_type=f32)
            val = val[: 2 * rows_own] + val[2 * rows_own :]
            vr_ = jnp.sum(jnp.where(hot_row, val[:rows_own], 0.0), 0, keepdims=True)
            vi_ = jnp.sum(jnp.where(hot_row, val[rows_own:], 0.0), 0, keepdims=True)
            return jnp.concatenate([vr_, vi_], 0)

        def body(t, carry):
            a = one(lo + 2 * t)
            b = one(lo + 2 * t + 1)
            vals[side, lo + 2 * t] = a
            vals[side, lo + 2 * t + 1] = b
            return carry

        lax.fori_loop(0, (hi - lo) // 2, body, 0)

    def back(d, to, slot):
        return pltpu.make_async_remote_copy(
            vals.at[h, to], slots.at[slot], ws.at[d], wr.at[d],
            device_id=device(to, h), device_id_type=MESH,
        )

    stage_two(0)
    gridding(h, 0, half)
    stage_two(1)
    gridding(h, half, chips)
    stage_three(0)
    land(k_vis, vis_all.at[1 - h])
    gridding(1 - h, 0, half)
    stage_three(1)
    gridding(1 - h, half, chips)
    turn(0)
    turn(1)
    degrid(1 - h, 0, half)
    stage_five(0)
    degrid(1 - h, half, chips)
    k_vals = send(vals.at[1 - h], pair_vals, sib)
    stage_five(1)
    degrid(h, 0, half)
    stage_six(0)
    degrid(h, half, chips)
    stage_six(1)
    land(k_vals, pair_vals)
    vals[h] = vals[h] + pair_vals[...]
    peers(lambda d, to, frm: back(d, to, me).start())
    finish(0)
    finish(1)
    peers(lambda d, to, frm: back(d, to, frm).wait_recv())
    start = vals[h, me]
    res_ref[...] = obs_ref[...] - lax.fori_loop(
        1, chips, lambda d, t: t + slots[lax.rem(me + d, chips)], start
    )
    for k, index in cross:
        land(k, g_ref.at[(1 - h,) + index])
    for copy in sent:
        copy.wait_send()
    peers(lambda d, to, frm: link(d, to, me).wait_send())
    peers(lambda d, to, frm: back(d, to, me).wait_send())


def main(ro, co, sub, u, v, obs, facet, scale):
    _, _, nx, ny, nz = geometry()
    chips = nx * ny * nz
    fs = facet.shape[0]
    nv = obs.shape[1]
    rows_own = NR * SG // chips
    long = nz * rows_own
    copies = 128
    dma = pltpu.SemaphoreType.DMA
    return pl.pallas_call(
        functools.partial(main_kernel, scale),
        out_shape=[
            jax.ShapeDtypeStruct((2, 2, 2, nx, ny, long, SG // 2), bf16),
            jax.ShapeDtypeStruct((NR * SG, 2 * fs), bf16),
            jax.ShapeDtypeStruct((NR * SG, 2 * fs), bf16),
            jax.ShapeDtypeStruct((NC, 2 * SG, fs), bf16),
            jax.ShapeDtypeStruct((2, nv), f32),
        ],
        in_specs=[SM, SM] + [VM] * 5,
        out_specs=[VM] * 5,
        scratch_shapes=[
            pltpu.VMEM((SG, SG), bf16),
            pltpu.VMEM((SG, SG), bf16),
            pltpu.VMEM((SG, 2 * fs), bf16),
            pltpu.VMEM((SG, 2 * fs), bf16),
            pltpu.VMEM((4, nv), f32),
            pltpu.VMEM((2, chips, 4, nv), f32),
            pltpu.VMEM((fs, fs), bf16),
            pltpu.VMEM((2, 2, nx, ny, long, SG // 2), f32),
            pltpu.VMEM((2, 2, nx, ny, long, SG // 2), bf16),
            pltpu.VMEM((5 * rows_own, SG), f32),
            pltpu.VMEM((2, ny, long, SG // 2), f32),
            pltpu.VMEM((2, nx, long, SG // 2), f32),
            pltpu.VMEM((2, ny, long, SG // 2), bf16),
            pltpu.VMEM((2, nx, long, SG // 2), bf16),
            pltpu.VMEM((2, nx - 1, ny, long, SG // 2), bf16),
            pltpu.VMEM((2, ny - 1, nx, long, SG // 2), bf16),
            pltpu.VMEM((2, ny - 1, long, SG // 2), bf16),
            pltpu.VMEM((2, nx - 1, long, SG // 2), bf16),
            pltpu.VMEM((2, nz, rows_own, SG), f32),
            pltpu.VMEM((2, nz, rows_own, SG), bf16),
            pltpu.VMEM((2, nz - 1, rows_own, SG), bf16),
            pltpu.VMEM((2, nz, rows_own, SG), bf16),
            pltpu.VMEM((4 * rows_own, SG), bf16),
            pltpu.VMEM((2, chips, 2, nv), f32),
            pltpu.VMEM((chips, 2, nv), f32),
            pltpu.VMEM((chips, 2, nv), f32),
            dma((copies,)),
            dma((copies,)),
            dma((chips,)),
            dma((chips,)),
            dma((chips,)),
            dma((chips,)),
            dma,
        ],
        compiler_params=pltpu.CompilerParams(
            collective_id=0, has_side_effects=True, vmem_limit_bytes=LIMIT
        ),
        name="cycle",
    )(ro, co, sub, u, v, obs, facet)


def backward_kernel(scale, g_ref, ar_ref, ai_ref, bt_ref, image_ref):
    _, h, _, _ = position()
    fs = image_ref.shape[0]
    cut = pl.ds(pl.multiple_of(h * fs, fs), fs)
    first = (((0,), (0,)), ((), ()))
    g = jnp.concatenate([g_ref[c, w, p] for c in range(NC) for p in range(2) for w in range(2)], 1)
    one = lax.dot_general(ar_ref[:, cut], g, first, preferred_element_type=f32)
    two = lax.dot_general(ai_ref[:, cut], g, first, preferred_element_type=f32)
    parts = []
    for c in range(NC):
        re = slice(2 * c * SG, (2 * c + 1) * SG)
        im = slice((2 * c + 1) * SG, (2 * c + 2) * SG)
        parts += [one[:, re] + two[:, im], one[:, im] - two[:, re]]
    u = jnp.concatenate(parts, 1).astype(bf16)
    b = bt_ref[...].reshape(2 * NC * SG, fs)
    image_ref[...] = jnp.dot(u, b, preferred_element_type=f32) * scale


def backward(g, ar, ai, bt, scale):
    fs = bt.shape[2]
    return pl.pallas_call(
        functools.partial(backward_kernel, scale),
        out_shape=jax.ShapeDtypeStruct((fs, fs), f32),
        in_specs=[VM] * 4,
        out_specs=VM,
        compiler_params=pltpu.CompilerParams(vmem_limit_bytes=LIMIT),
        name="backward",
    )(g, ar, ai, bt)


def shards(facet_image, row_offsets, col_offsets, vis_subgrid, vis_u, vis_v, observed):
    rows, cols, _, _, _ = geometry()
    fs = facet_image.shape[0]
    scale_in = 1.0 / (fs * math.sqrt(rows * cols))
    scale_out = 1.0 / (SG * math.sqrt(NR * NC))
    g, ar, ai, bt, residual = main(
        row_offsets, col_offsets, vis_subgrid[None], vis_u[None], vis_v[None],
        observed, facet_image, scale_in / SG,
    )
    image = backward(g.reshape(NC, 2, 2, NR * SG, SG // 2), ar, ai, bt, scale_out / SG)
    return (image, residual)


def solution(mesh):
    in_specs = (
        P("frow", "fcol"),
        P(),
        P(),
        P(("frow", "fcol")),
        P(("frow", "fcol")),
        P(("frow", "fcol")),
        P(None, ("frow", "fcol")),
    )
    out_specs = (P("frow", "fcol"), P(None, ("frow", "fcol")))
    return jax.shard_map(shards, mesh=mesh, in_specs=in_specs, out_specs=out_specs, check_vma=False)
```
